256 devices in a mesh: seq: 32 (over z_hi, x, core), head: 8 (over y, z_lo).
Axes of the slice: x: 4, y: 4, z: 8 (z_hi: 4, z_lo: 2; z = z_hi * 2 + z_lo), core: 2. Of those that a mesh axis runs over, the one named last changes fastest.
Arguments:
- queries: bfloat16 [24576, 4096], P('seq', 'head'), may hold values from -100 to 100
- keys: bfloat16 [24576, 4096], P('seq', 'head'), may hold values from -7 to 7
- values: bfloat16 [24576, 4096], P('seq', 'head'), may hold values from -6 to 6
- targets: bfloat16 [24576, 4096], P('seq', 'head'), may hold values from -6 to 6
- token_rate: float32 [24576, 8], P('seq', 'head'), may hold values from 0.1 to 1
- window: int32 [8], P('head'), may hold values from 256 to 512, as said below
- split: int32 [1], replicated, may hold values from 9216 to 15359
- fast_init: float32 [8, 3, 512, 512], P('head'), may hold values from -0.25 to 0.25
Outputs:
- mixed: bfloat16 [24576, 4096], P('seq', 'head')
- fast_final: float32 [8, 3, 512, 512], P('head')
The draws below stay inside these ranges and needn't reach their ends.
Inputs may be any that keep to these rules, and one draw needn't show every extreme that they name: Some head has a window of exactly 512.
All inputs are finite; a program needn't handle non-finite values.
Results may differ from the reference program's by a relative error of at most 0.0073.
Values may be sent and summed in bfloat16 or wider, within the bound.
No kernel may reach another device: no remote copies, remote signals or barrier semaphores. Data moves between devices by JAX's collectives and lax.ppermute only.
A program may use at most 64 MiB of HBM per device.

```python
import math
import jax
import jax.numpy as jnp
from jax import lax

HEADS = 8
HD = 512
HID = 512
WIN = 512
TOKENS = 24576


def joint_draw(key):
    base = jax.random.fold_in(key, 11)
    key_a, key_b = jax.random.split(base, 2)
    shape = (TOKENS, HEADS * HD)
    keys = jax.random.truncated_normal(key_a, -6.0, 6.0, shape, jnp.float32)
    queries = jax.random.truncated_normal(key_b, -6.0, 6.0, shape, jnp.float32)
    return (queries, keys)


def draw_queries(key, part):
    return joint_draw(key)[0].astype(jnp.bfloat16)


def draw_keys(key, part):
    return joint_draw(key)[1].astype(jnp.bfloat16)


def draw_window(key, part):
    base = jax.random.fold_in(key, 23)
    key_a, key_b = jax.random.split(base)
    widths = jax.random.randint(key_a, (HEADS,), WIN // 2, WIN + 1)
    chosen = jax.random.randint(key_b, (), 0, HEADS)
    return jnp.where(jnp.arange(HEADS) == chosen, WIN, widths).astype(jnp.int32)


def block_levels(stream_key, extent, cuts, low, high):
    loudness = 1.0
    for axis_at, parts in cuts:
        draws = jax.random.uniform(jax.random.fold_in(jax.random.fold_in(stream_key, 6), axis_at), (parts,), jnp.float32, low / len(cuts), high / len(cuts))
        loudness = loudness * jnp.repeat(jnp.exp(draws), extent[axis_at] // parts).reshape((-1,) + (1,) * (len(extent) - 1 - axis_at))
    return loudness


def bell_draw(key, shape, spread, most, pieces=(), kind=jnp.bfloat16):
    values = spread * jax.random.normal(key, shape, jnp.float32)
    if pieces:
        values = values * block_levels(key, shape, pieces, -0.22, 0.18)
    return jnp.clip(values, -most, most).astype(kind)


def setup_inputs(seed: int = 0) -> dict:
    seeds = jax.random.split(jax.random.key(seed), 9)
    return {
        "queries": draw_queries(jax.random.fold_in(seeds[8], 71), 0),
        "keys": draw_keys(jax.random.fold_in(seeds[8], 71), 0),
        "values": bell_draw(seeds[2], (TOKENS, HEADS * HD), 1.0, 6.0, ((0, 32), (1, 8))),
        "targets": bell_draw(seeds[3], (TOKENS, HEADS * HD), 1.0, 6.0, ((0, 32), (1, 8))),
        "token_rate": jnp.clip(jnp.exp(math.log(1.0) - 2.3025851 * jax.random.uniform(seeds[4], (TOKENS, HEADS), jnp.float32) ** block_levels(seeds[4], (TOKENS, HEADS), ((0, 32), (1, 8)), -0.2, 0.2)), 0.1, 1.0),
        "window": draw_window(jax.random.fold_in(seeds[8], 71), 0),
        "split": jax.random.randint(seeds[6], (1,), TOKENS // 2 - TOKENS // 8, TOKENS // 2 + TOKENS // 8).astype(jnp.int32),
        "fast_init": bell_draw(seeds[7], (HEADS, 3, HD, HID), HD ** -0.5, 0.25, ((0, 8),), jnp.float32),
    }


fast_rate = 0.01
epsilon = 1e-06

def fast_apply(inputs, weights):
    first = jnp.dot(inputs, weights[0], preferred_element_type=jnp.float32)
    third = jnp.dot(inputs, weights[1], preferred_element_type=jnp.float32)
    act = (jax.nn.silu(first) * third).astype(jnp.bfloat16)
    return lax.dot_general(act, weights[2], (((1,), (1,)), ((), ())), preferred_element_type=jnp.float32)

def fast_grad(inputs, targets, scaled, weights):
    first = jnp.dot(inputs, weights[0], preferred_element_type=jnp.float32)
    third = jnp.dot(inputs, weights[1], preferred_element_type=jnp.float32)
    sigma = jax.nn.sigmoid(first)
    swish = first * sigma
    act = (swish * third).astype(jnp.bfloat16)
    d_out = (-scaled * targets.astype(jnp.float32)).astype(jnp.bfloat16)
    d_act = jnp.dot(d_out, weights[2], preferred_element_type=jnp.float32)
    d_first = (d_act * third * sigma * (1.0 + first * (1.0 - sigma))).astype(jnp.bfloat16)
    d_third = (d_act * swish).astype(jnp.bfloat16)
    dims = (((0,), (0,)), ((), ()))
    grad_one = lax.dot_general(inputs, d_first, dims, preferred_element_type=jnp.float32)
    grad_three = lax.dot_general(inputs, d_third, dims, preferred_element_type=jnp.float32)
    grad_two = lax.dot_general(d_out, act, dims, preferred_element_type=jnp.float32)
    return jnp.stack([grad_one, grad_three, grad_two])

def attend_head(query_head, key_head, value_head, width):
    total = query_head.shape[0]
    block = math.gcd(total, 512)
    pad = jnp.zeros((WIN, HD), jnp.bfloat16)
    key_pad = jnp.concatenate([pad, key_head], axis=0)
    value_pad = jnp.concatenate([pad, value_head], axis=0)
    scale = HD ** (-0.5)

    def one_block(start):
        query_block = lax.dynamic_slice_in_dim(query_head, start, block, 0)
        key_block = lax.dynamic_slice_in_dim(key_pad, start, block + WIN, 0)
        value_block = lax.dynamic_slice_in_dim(value_pad, start, block + WIN, 0)
        scores = lax.dot_general(query_block, key_block, (((1,), (1,)), ((), ())), preferred_element_type=jnp.float32) * scale
        query_pos = start + jnp.arange(block, dtype=jnp.int32)[:, None]
        key_pos = start - WIN + jnp.arange(block + WIN, dtype=jnp.int32)[None, :]
        live = (key_pos <= query_pos) & (key_pos > query_pos - width) & (key_pos >= 0)
        scores = jnp.where(live, scores, -1e+30)
        peak = lax.optimization_barrier(jnp.max(scores, axis=1, keepdims=True))
        expo = jnp.where(live, jnp.exp(scores - peak), 0.0)
        probs = (expo / lax.optimization_barrier(jnp.sum(expo, axis=1, keepdims=True))).astype(jnp.bfloat16)
        return jnp.dot(probs, value_block, preferred_element_type=jnp.float32)
    starts = jnp.arange(total // block, dtype=jnp.int32) * block
    return lax.map(one_block, starts).reshape(total, HD)

def renew_weights(weights, grads):
    square = jnp.sum(grads * grads)
    count = float(HEADS * 3 * HD * HID)
    return weights - fast_rate / jnp.sqrt(square / count + epsilon) * grads

def reference(queries, keys, values, targets, token_rate, window, split, fast_init):
    positions = jnp.arange(TOKENS, dtype=jnp.int32)[:, None]
    first_block = (positions < split[0]).astype(jnp.float32)
    second_block = 1.0 - first_block

    def column(array, head):
        return lax.dynamic_slice_in_dim(array, head * HD, HD, 1)

    def grads_of(weights, mask):

        def per_head(head):
            scaled = lax.dynamic_slice_in_dim(token_rate, head, 1, 1) * mask
            return fast_grad(column(keys, head), column(targets, head), scaled, weights[head].astype(jnp.bfloat16))
        return lax.map(per_head, jnp.arange(HEADS, dtype=jnp.int32))
    weights_zero = fast_init
    weights_one = renew_weights(weights_zero, grads_of(weights_zero, first_block))
    weights_two = renew_weights(weights_one, grads_of(weights_one, second_block))

    def output_head(head):
        query_head = column(queries, head)
        attn = attend_head(query_head, column(keys, head), column(values, head), window[head])
        early = fast_apply(query_head, weights_zero[head].astype(jnp.bfloat16))
        late = fast_apply(query_head, weights_one[head].astype(jnp.bfloat16))
        fast_out = first_block * early + second_block * late
        normed = fast_out / jnp.sqrt(lax.optimization_barrier(jnp.mean(fast_out * fast_out, axis=1, keepdims=True)) + epsilon)
        return (attn + normed).astype(jnp.bfloat16)
    heads_out = lax.map(output_head, jnp.arange(HEADS, dtype=jnp.int32))
    mixed = jnp.transpose(heads_out, (1, 0, 2)).reshape(TOKENS, HEADS * HD)
    return (mixed, weights_two)
```

```python
import math

import jax
import jax.numpy as jnp
from jax import lax
from jax.sharding import Mesh
from jax.sharding import PartitionSpec as P

HEADS = 8
HD = 512
HID = 512
WIN = 512
ROWS = 3 * HD
SEQ = ("z", "x", "core")

fast_rate = 0.01
epsilon = 1e-06
bf16 = jnp.bfloat16
f32 = jnp.float32


def exchange(value, mesh_axes, partner):
    count = math.prod(lax.axis_size(a) for a in mesh_axes)
    return lax.ppermute(value, mesh_axes, [(i, partner(i)) for i in range(count)])


def ring_pair(step):
    def partner(i):
        place, core = divmod(i, 2)
        return (place ^ (1 if core == step else 3)) * 2 + core

    return partner


def swap_x(value, step):
    return exchange(value, ("x", "core"), ring_pair(step))


def swap_z(value, step):
    return exchange(value, ("z", "core"), ring_pair(step))


def swap_core(value):
    return exchange(value, ("core",), lambda i: i ^ 1)


def swap_head(value, bits):
    return exchange(value, ("head",), lambda i: i ^ bits)


def part(value, index):
    half = value.shape[0] // 2
    return lax.dynamic_slice_in_dim(value, index * half, half, 0)


def joined(own, other, bit):
    half = own.shape[0]
    whole = jnp.zeros((2 * half, own.shape[1]), own.dtype)
    whole = lax.dynamic_update_slice_in_dim(whole, own, bit * half, 0)
    return lax.dynamic_update_slice_in_dim(whole, other, (1 - bit) * half, 0)


def summed_over_seq(grad):
    core = lax.axis_index("core")
    place = lax.axis_index("x")
    low, high = place & 1, place >> 1
    first = jnp.where(core == 0, low ^ high, high)
    second = jnp.where(core == 0, high, low ^ high)

    got = swap_core(part(grad, 1 - core).astype(bf16))
    own = part(grad, core)
    got_x = swap_x((part(own, 1 - first) + part(got, 1 - first).astype(f32)).astype(bf16), 0)
    own = part(own, first) + part(got, first).astype(f32)
    got_x2 = swap_x((part(own, 1 - second) + part(got_x, 1 - second).astype(f32)).astype(bf16), 1)
    own = part(own, second) + part(got_x, second).astype(f32) + got_x2.astype(f32)
    for step in range(2):
        own = own.astype(bf16)
        own = own.astype(f32) + swap_z(own, step).astype(f32)

    square = jnp.broadcast_to(jnp.sum(own * own), (8, 128))
    square = square + swap_head(square, 2)
    square = square + swap_head(square, 6)
    square = square + swap_head(square, 1)
    square = square + swap_x(square, 1)
    square = square + swap_x(square, 0)
    square = square + swap_core(square)

    total = own.astype(bf16)
    total = joined(total, swap_x(total, 1), second)
    total = joined(total, swap_x(total, 0), first)
    total = joined(total, swap_core(total), core)
    return total, square[0, 0]


def fast_apply(inputs, weights):
    first = jnp.dot(inputs, weights[0], preferred_element_type=f32)
    third = jnp.dot(inputs, weights[1], preferred_element_type=f32)
    act = (jax.nn.silu(first) * third).astype(bf16)
    return lax.dot_general(act, weights[2], (((1,), (1,)), ((), ())), preferred_element_type=f32)


def fast_grad(inputs, targets, scaled, weights):
    first = jnp.dot(inputs, weights[0], preferred_element_type=f32)
    third = jnp.dot(inputs, weights[1], preferred_element_type=f32)
    sigma = jax.nn.sigmoid(first)
    swish = first * sigma
    act = (swish * third).astype(bf16)
    d_out = (-scaled * targets.astype(f32)).astype(bf16)
    d_act = jnp.dot(d_out, weights[2], preferred_element_type=f32)
    d_first = (d_act * third * sigma * (1.0 + first * (1.0 - sigma))).astype(bf16)
    d_third = (d_act * swish).astype(bf16)
    dims = (((0,), (0,)), ((), ()))
    grad_one = lax.dot_general(inputs, d_first, dims, preferred_element_type=f32)
    grad_three = lax.dot_general(inputs, d_third, dims, preferred_element_type=f32)
    grad_two = lax.dot_general(d_out, act, dims, preferred_element_type=f32)
    return jnp.concatenate([grad_one, grad_three, grad_two], axis=0)


def attend_head(query_head, key_ext, value_ext, width, anchor):
    local = query_head.shape[0]
    block = math.gcd(local, 512)
    scale = HD ** (-0.5)
    done = []
    for start in range(0, local, block):
        query_block = query_head[start : start + block]
        key_block = key_ext[start : start + block + WIN]
        value_block = value_ext[start : start + block + WIN]
        scores = lax.dot_general(query_block, key_block, (((1,), (1,)), ((), ())), preferred_element_type=f32) * scale
        query_pos = anchor + start + jnp.arange(block, dtype=jnp.int32)[:, None]
        key_pos = anchor + start - WIN + jnp.arange(block + WIN, dtype=jnp.int32)[None, :]
        live = (key_pos <= query_pos) & (key_pos > query_pos - width) & (key_pos >= 0)
        scores = jnp.where(live, scores, -1e30)
        peak = jnp.max(scores, axis=1, keepdims=True)
        expo = jnp.where(live, jnp.exp(scores - peak), 0.0)
        probs = (expo / jnp.sum(expo, axis=1, keepdims=True)).astype(bf16)
        done.append(jnp.dot(probs, value_block, preferred_element_type=f32))
    return jnp.concatenate(done, axis=0)


def per_device(queries, keys, values, targets, token_rate, window, split, fast_init):
    local = queries.shape[0]
    anchor = lax.axis_index(SEQ) * local
    count = lax.axis_size(SEQ)
    onward = [(i, i + 1) for i in range(count - 1)]
    key_ext = jnp.concatenate([lax.ppermute(keys[local - WIN :], SEQ, onward), keys], axis=0)
    value_ext = jnp.concatenate([lax.ppermute(values[local - WIN :], SEQ, onward), values], axis=0)
    positions = anchor + jnp.arange(local, dtype=jnp.int32)[:, None]
    first_block = (positions < split[0]).astype(f32)
    second_block = 1.0 - first_block

    def renewed(weights, mask):
        grad = fast_grad(keys, targets, token_rate * mask, weights.reshape(3, HD, HID).astype(bf16))
        total, square = summed_over_seq(grad)
        factor = fast_rate / jnp.sqrt(square / float(HEADS * ROWS * HID) + epsilon)
        return weights - factor * total.astype(f32)

    weights_zero = fast_init.reshape(ROWS, HID)
    weights_one = renewed(weights_zero, first_block)
    weights_two = renewed(weights_one, second_block)
    attn = attend_head(queries, key_ext, value_ext, window[0], anchor)
    early = fast_apply(queries, weights_zero.reshape(3, HD, HID).astype(bf16))
    late = fast_apply(queries, weights_one.reshape(3, HD, HID).astype(bf16))
    fast_out = first_block * early + second_block * late
    normed = fast_out / jnp.sqrt(jnp.mean(fast_out * fast_out, axis=1, keepdims=True) + epsilon)
    outputs = (attn + normed).astype(bf16)
    return (outputs, weights_two.reshape(1, 3, HD, HID))


def solution(mesh):
    finer = Mesh(mesh.devices.reshape(4, 4, 2, mesh.shape["head"]), ("z", "x", "core", "head"))
    tokens = P(SEQ, "head")
    weights = P("head", None, None, None)
    return jax.shard_map(
        per_device,
        mesh=finer,
        in_specs=(tokens,) * 5 + (P("head"), P(), weights),
        out_specs=(tokens, weights),
        check_vma=False,
    )
```

```python
import functools
import math

import jax
import jax.numpy as jnp
from jax import lax
from jax.experimental import pallas as pl
from jax.experimental.pallas import tpu as pltpu
from jax.sharding import Mesh
from jax.sharding import PartitionSpec as P

HEADS = 8
HD = 512
HID = 512
WIN = 512
ROWS = 3 * HD
SEQ = ("z", "x", "core")
TILE = 256

fast_rate = 0.01
epsilon = 1e-06
bf16 = jnp.bfloat16
f32 = jnp.float32
VMEM_SPEC = pl.BlockSpec(memory_space=pltpu.VMEM)
SMEM_SPEC = pl.BlockSpec(memory_space=pltpu.SMEM)
PARAMS = pltpu.CompilerParams(vmem_limit_bytes=48 << 20)


def dot(a, b, over_a, over_b):
    return lax.dot_general(a, b, (((over_a,), (over_b,)), ((), ())), preferred_element_type=f32)


def exchange(value, mesh_axes, partner):
    count = math.prod(lax.axis_size(a) for a in mesh_axes)
    return lax.ppermute(value, mesh_axes, [(i, partner(i)) for i in range(count)])


def ring_pair(step):
    def partner(i):
        place, core = divmod(i, 2)
        return (place ^ (1 if core == step else 3)) * 2 + core

    return partner


def swap_x(value, step):
    return exchange(value, ("x", "core"), ring_pair(step))


def swap_z(value, step):
    return exchange(value, ("z", "core"), ring_pair(step))


def swap_core(value):
    return exchange(value, ("core",), lambda i: i ^ 1)


def swap_head(value, bits):
    return exchange(value, ("head",), lambda i: i ^ bits)


def of_four(value, swap):
    return (value + swap(value, 1)) + (swap(value, 2) + swap(value, 3))


def summed_squares(value):
    square = jnp.broadcast_to(jnp.sum(value * value), (8, 128))
    square = square + swap_core(square)
    square = of_four(square, lambda v, k: swap_head(v, 2 * k))
    square = of_four(square, lambda v, k: exchange(v, ("x",), lambda i: i ^ k))
    square = square + swap_head(square, 1)
    return square[0, 0].reshape(1)


def part(value, index):
    half = value.shape[0] // 2
    return lax.dynamic_slice_in_dim(value, index * half, half, 0)


def halves():
    core = lax.axis_index("core")
    place = lax.axis_index("x")
    low, high = place & 1, place >> 1
    first = jnp.where(core == 0, low ^ high, high)
    second = jnp.where(core == 0, high, low ^ high)
    return core, first, second


def piece_starts():
    core, a, b = halves()
    here = [(a, b), (a, 1 - b), (1 - a, b), (1 - a, 1 - b)]
    there = [(b, a), (b, 1 - a), (1 - b, a), (1 - b, 1 - a)]
    places = [core * 4 + i * 2 + j for i, j in here] + [(1 - core) * 4 + i * 2 + j for i, j in there]
    return (jnp.stack(places) * (ROWS // 8)).astype(jnp.int32)


def reduced(sent, own, beside=None):
    _, first, second = halves()
    got = swap_core(sent)
    got_x = swap_x((part(own, 1 - first) + part(got, 1 - first).astype(f32)).astype(bf16), 0)
    own = part(own, first) + part(got, first).astype(f32)
    got_x2 = swap_x((part(own, 1 - second) + part(got_x, 1 - second).astype(f32)).astype(bf16), 1)
    own = part(own, second) + part(got_x, second).astype(f32) + got_x2.astype(f32)
    own = own.astype(bf16)
    other = swap_z(own, 0)
    done = None
    if beside is not None:
        done, other = beside(own, other)
    own = (own.astype(f32) + other.astype(f32)).astype(bf16)
    return own.astype(f32) + swap_z(own, 1).astype(f32), done


def gathered(own):
    near = swap_x(own, 1)
    far = swap_x(own, 0)
    both = swap_x(near, 0)
    here = [own, near, far, both]
    return here + [swap_core(v) for v in here]


def grads(place, keys_ref, targets_ref, rate_ref, wb_ref, grad_ref, send_ref, keep_ref):
    keys = keys_ref[...]
    first = dot(keys, wb_ref[0:HD], 1, 0)
    third = dot(keys, wb_ref[HD : 2 * HD], 1, 0)
    d_out = (-rate_ref[...] * targets_ref[...].astype(f32)).astype(bf16)
    d_act = dot(d_out, wb_ref[2 * HD :], 1, 0)
    sigma = jax.nn.sigmoid(first)
    swish = first * sigma
    act = (swish * third).astype(bf16)
    d_first = (d_act * third * sigma * (1.0 + first * (1.0 - sigma))).astype(bf16)
    d_third = (d_act * swish).astype(bf16)
    grad_ref[0:HD] = dot(keys, d_first, 0, 0)
    grad_ref[HD : 2 * HD] = dot(keys, d_third, 0, 0)
    grad_ref[2 * HD :] = dot(d_out, act, 0, 0)
    half = ROWS // 2
    send_ref[...] = grad_ref[pl.ds(pl.multiple_of((1 - place) * half, half), half)].astype(bf16)
    keep_ref[...] = grad_ref[pl.ds(pl.multiple_of(place * half, half), half)]


def first_kernel(place_ref, keys_ref, targets_ref, rate_ref, w_ref, wb_ref, send_ref, keep_ref, grad_ref):
    wb_ref[...] = w_ref[...].astype(bf16)
    grads(place_ref[0], keys_ref, targets_ref, rate_ref, wb_ref, grad_ref, send_ref, keep_ref)


def renew(starts_ref, square_ref, w_ref, pieces, new_ref, wb_ref=None):
    mean = jnp.full((1, HID), square_ref[0] / float(HEADS * ROWS * HID), f32)
    factor = fast_rate / jnp.sqrt(mean + epsilon)
    rows = ROWS // 8
    for i, piece in enumerate(pieces):
        at = pl.ds(pl.multiple_of(starts_ref[i], rows), rows)
        new = w_ref[at] - factor * piece[...].astype(f32)
        new_ref[at] = new
        if wb_ref is not None:
            wb_ref[at] = new.astype(bf16)


def second_kernel(place_ref, starts_ref, square_ref, keys_ref, targets_ref, rate_ref, w_ref, *rest):
    pieces, (new_ref, wb_ref, send_ref, keep_ref, grad_ref) = rest[:8], rest[8:]
    renew(starts_ref, square_ref, w_ref, pieces, new_ref, wb_ref)
    grads(place_ref[0], keys_ref, targets_ref, rate_ref, wb_ref, grad_ref, send_ref, keep_ref)


def last_kernel(starts_ref, square_ref, w_ref, *rest):
    renew(starts_ref, square_ref, w_ref, rest[:8], rest[8])


def attend_kernel(meta_ref, q_ref, halo_k_ref, k_ref, halo_v_ref, v_ref, out_ref):
    local = q_ref.shape[0]
    anchor, width = meta_ref[0], meta_ref[1]
    scale = HD ** (-0.5)
    for start in range(0, local, TILE):
        spans = []
        if start < WIN:
            spans.append((halo_k_ref, halo_v_ref, start, WIN, start - WIN))
        spans.append((k_ref, v_ref, max(start - WIN, 0), start + TILE, 0))
        query = q_ref[start : start + TILE]
        scores = []
        for keys, _, low, high, base in spans:
            s = dot(query, keys[low:high], 1, 1) * scale
            row = lax.broadcasted_iota(jnp.int32, s.shape, 0) + start
            col = lax.broadcasted_iota(jnp.int32, s.shape, 1) + (low - WIN if base else low)
            live = (col <= row) & (col > row - width) & (col >= -anchor)
            scores.append(jnp.where(live, s, -1e30))
        peak = functools.reduce(jnp.maximum, [jnp.max(s, axis=1, keepdims=True) for s in scores])
        expo = [jnp.exp(s - peak) for s in scores]
        total = sum(jnp.sum(e, axis=1, keepdims=True) for e in expo)
        inverse = 1.0 / total
        attn = 0.0
        for e, (_, values, low, high, _) in zip(expo, spans):
            attn = attn + dot((e * inverse).astype(bf16), values[low:high], 1, 0)
        out_ref[start : start + TILE] = attn


def apply_kernel(meta_ref, q_ref, attn_ref, early_ref, late_ref, out_ref, y_ref):
    anchor, split = meta_ref[0], meta_ref[2]

    def fast(query, wb_ref):
        first = dot(query, wb_ref[0:HD], 1, 0)
        third = dot(query, wb_ref[HD : 2 * HD], 1, 0)
        act = (first * jax.nn.sigmoid(first) * third).astype(bf16)
        return dot(act, wb_ref[2 * HD :], 1, 1)

    for start in range(0, q_ref.shape[0], TILE):
        rows = slice(start, start + TILE)

        @pl.when(anchor + start < split)
        def _():
            y_ref[...] = fast(q_ref[rows], early_ref)

        @pl.when(anchor + start + TILE > split)
        def _():
            late = fast(q_ref[rows], late_ref)
            position = anchor + start + lax.broadcasted_iota(jnp.int32, late.shape, 0)
            y_ref[...] = jnp.where(position < split, y_ref[...], late)

        y = y_ref[...]
        norm = y / jnp.sqrt(jnp.mean(y * y, axis=1, keepdims=True) + epsilon)
        out_ref[rows] = (attn_ref[rows] + norm).astype(bf16)


def call(kernel, specs, outs, args, scratch=()):
    return pl.pallas_call(
        kernel,
        out_shape=outs,
        in_specs=specs,
        out_specs=jax.tree.map(lambda _: VMEM_SPEC, outs),
        scratch_shapes=list(scratch),
        compiler_params=PARAMS,
    )(*args)


def array(shape, dtype):
    return jax.ShapeDtypeStruct(shape, dtype)


def per_device(queries, keys, values, targets, token_rate, window, split, fast_init):
    local = queries.shape[0]
    anchor = lax.axis_index(SEQ) * local
    count = lax.axis_size(SEQ)
    onward = [(i, i + 1) for i in range(count - 1)]
    halo_k = lax.ppermute(keys[local - WIN :], SEQ, onward)
    halo_v = lax.ppermute(values[local - WIN :], SEQ, onward)
    positions = anchor + jnp.arange(local, dtype=jnp.int32)[:, None]
    first_block = (positions < split[0]).astype(f32)
    rate_zero = token_rate * first_block
    rate_one = token_rate * (1.0 - first_block)
    core = lax.axis_index("core").astype(jnp.int32).reshape(1)
    starts = piece_starts()
    meta = jnp.stack([anchor, window[0], split[0]]).astype(jnp.int32)
    weights_zero = fast_init.reshape(ROWS, HID)
    half = ROWS // 2
    wide = [array((half, HID), bf16), array((half, HID), f32)]
    scratch = [pltpu.VMEM((ROWS, HID), f32)]

    wb_zero, sent, own = call(
        first_kernel,
        [SMEM_SPEC] + [VMEM_SPEC] * 4,
        [array((ROWS, HID), bf16)] + wide,
        (core, keys, targets, rate_zero, weights_zero),
        scratch,
    )

    def attend(before, after):
        query, _ = lax.optimization_barrier((queries, before))
        attn = call(
            attend_kernel,
            [SMEM_SPEC] + [VMEM_SPEC] * 5,
            array((local, HD), f32),
            (meta, query, halo_k, keys, halo_v, values),
        )
        return lax.optimization_barrier((attn, after))

    total, attn = reduced(sent, own, attend)
    square = summed_squares(total)
    pieces = gathered(total.astype(bf16))
    weights_one, wb_one, sent, own = call(
        second_kernel,
        [SMEM_SPEC] * 3 + [VMEM_SPEC] * 12,
        [array((ROWS, HID), f32), array((ROWS, HID), bf16)] + wide,
        (core, starts, square, keys, targets, rate_one, weights_zero, *pieces),
        scratch,
    )

    def apply(before, after):
        query, _ = lax.optimization_barrier((queries, before))
        outputs = call(
            apply_kernel,
            [SMEM_SPEC] + [VMEM_SPEC] * 4,
            array((local, HD), bf16),
            (meta, query, attn, wb_zero, wb_one),
            [pltpu.VMEM((TILE, HD), f32)],
        )
        return lax.optimization_barrier((outputs, after))

    total, outputs = reduced(sent, own, apply)
    square = summed_squares(total)
    pieces = gathered(total.astype(bf16))
    weights_two = call(
        last_kernel,
        [SMEM_SPEC] * 2 + [VMEM_SPEC] * 9,
        array((ROWS, HID), f32),
        (starts, square, weights_one, *pieces),
    )
    return (outputs, weights_two.reshape(1, 3, HD, HID))


def solution(mesh):
    finer = Mesh(mesh.devices.reshape(4, 4, 2, mesh.shape["head"]), ("z", "x", "core", "head"))
    tokens = P(SEQ, "head")
    weights = P("head", None, None, None)
    return jax.shard_map(
        per_device,
        mesh=finer,
        in_specs=(tokens,) * 5 + (P("head"), P(), weights),
        out_specs=(tokens, weights),
        check_vma=False,
    )
```

```python
import functools
import math

import jax
import jax.numpy as jnp
from jax import lax
from jax.experimental import pallas as pl
from jax.experimental.pallas import tpu as pltpu
from jax.sharding import Mesh
from jax.sharding import PartitionSpec as P

HEADS = 8
HD = 512
HID = 512
WIN = 512
ROWS = 3 * HD
SEQ = ("z", "x", "core")
TILE = 256
CHUNKS = 2

fast_rate = 0.01
epsilon = 1e-06
bf16 = jnp.bfloat16
f32 = jnp.float32
VMEM_SPEC = pl.BlockSpec(memory_space=pltpu.VMEM)
SMEM_SPEC = pl.BlockSpec(memory_space=pltpu.SMEM)
ANY_SPEC = pl.BlockSpec(memory_space=pl.ANY)


def dot(a, b, over_a, over_b):
    return lax.dot_general(a, b, (((over_a,), (over_b,)), ((), ())), preferred_element_type=f32)


def exchange(value, mesh_axes, partner):
    count = math.prod(lax.axis_size(a) for a in mesh_axes)
    return lax.ppermute(value, mesh_axes, [(i, partner(i)) for i in range(count)])


def ring_pair(step):
    def partner(i):
        place, core = divmod(i, 2)
        return (place ^ (1 if core == step else 3)) * 2 + core

    return partner


def swap_x(value, step):
    return exchange(value, ("x", "core"), ring_pair(step))


def swap_z(value, step):
    return exchange(value, ("z", "core"), ring_pair(step))


def swap_core(value):
    return exchange(value, ("core",), lambda i: i ^ 1)


def swap_head(value, bits):
    return exchange(value, ("head",), lambda i: i ^ bits)


def of_four(value, swap):
    return (value + swap(value, 1)) + (swap(value, 2) + swap(value, 3))


def over_seq_and_head(square):
    square = of_four(square, lambda v, k: exchange(v, ("core", "head"), lambda i: i ^ (0, 1, 8, 9)[k]))
    square = of_four(square, lambda v, k: swap_head(v, 2 * k))
    square = of_four(square, lambda v, k: exchange(v, ("x",), lambda i: i ^ k))
    return square


def rows_of(value, start, count):
    return lax.dynamic_slice_in_dim(value, start, count, 0)


def halves():
    core = lax.axis_index("core")
    place = lax.axis_index("x")
    low, high = place & 1, place >> 1
    first = jnp.where(core == 0, low ^ high, high)
    second = jnp.where(core == 0, high, low ^ high)
    return core, first, second


def piece_starts():
    core, a, b = halves()
    here = [(a, b), (a, 1 - b), (1 - a, b), (1 - a, 1 - b)]
    there = [(b, a), (b, 1 - a), (1 - b, a), (1 - b, 1 - a)]
    places = [core * 4 + i * 2 + j for i, j in here] + [(1 - core) * 4 + i * 2 + j for i, j in there]
    return (jnp.stack(places) * (ROWS // 8)).astype(jnp.int32)


def reduced(sent, own, beside_first=None, beside_second=None):
    _, first, second = halves()
    half, rows = ROWS // 4, ROWS // 8
    chunks = range(len(sent))
    got = [swap_core(s) for s in sent]

    def two(c, start, count):
        return rows_of(own[c], start, count) + rows_of(got[c], start, count).astype(f32)

    got_x = [swap_x(two(c, (1 - first) * half, half).astype(bf16), 0) for c in chunks]
    away = (1 - second) * rows
    send = [(two(c, first * half + away, rows) + rows_of(got_x[c], away, rows).astype(f32)).astype(bf16) for c in chunks]
    got_x2 = [swap_x(s, 1) for s in send]
    near = second * rows
    mine = [two(c, first * half + near, rows) + rows_of(got_x[c], near, rows).astype(f32) + got_x2[c].astype(f32) for c in chunks]
    mine = [m.astype(bf16) for m in mine]
    other = [swap_z(m, 0) for m in mine]
    if beside_first is not None:
        other = beside_first(mine, other)
    mine = [(m.astype(f32) + o.astype(f32)).astype(bf16) for m, o in zip(mine, other)]
    other = [swap_z(m, 1) for m in mine]
    if beside_second is not None:
        other = beside_second(mine, other)
    return mine, other


def gathered(own):
    near = swap_x(own, 1)
    pair = jnp.concatenate([own, near], axis=0)
    far = swap_x(pair, 0)
    return [pair, far, swap_core(pair), swap_core(far)]


def finish_kernel(*refs):
    total_ref, square_ref = refs[2 * CHUNKS :]
    wide = HID // CHUNKS
    for c in range(CHUNKS):
        total = refs[c][...].astype(f32) + refs[CHUNKS + c][...].astype(f32)
        total_ref[:, c * wide : (c + 1) * wide] = total.astype(bf16)
        square = jnp.sum(total * total, axis=0, keepdims=True)
        square = square if c == 0 else before + square
        before = square
    square_ref[...] = jnp.broadcast_to(jnp.sum(square, axis=1, keepdims=True), (8, 128))


def grads(place, keys_ref, targets_ref, rate_ref, wb_ref, grad_ref, outs):
    keys = keys_ref[...]
    d_out = (-rate_ref[...] * targets_ref[...].astype(f32)).astype(bf16)
    half, wide = ROWS // 2, HID // CHUNKS
    for c in range(CHUNKS):
        cols = slice(c * wide, (c + 1) * wide)
        first = dot(keys, wb_ref[0:HD, cols], 1, 0)
        third = dot(keys, wb_ref[HD : 2 * HD, cols], 1, 0)
        d_act = dot(d_out, wb_ref[2 * HD :, cols], 1, 0)
        sigma = jax.nn.sigmoid(first)
        swish = first * sigma
        act = (swish * third).astype(bf16)
        d_first = (d_act * third * sigma * (1.0 + first * (1.0 - sigma))).astype(bf16)
        d_third = (d_act * swish).astype(bf16)
        grad_ref[0:HD] = dot(keys, d_first, 0, 0)
        grad_ref[HD : 2 * HD] = dot(keys, d_third, 0, 0)
        grad_ref[2 * HD :] = dot(d_out, act, 0, 0)
        outs[c][...] = grad_ref[pl.ds(pl.multiple_of((1 - place) * half, half), half)].astype(bf16)
        outs[CHUNKS + c][...] = grad_ref[pl.ds(pl.multiple_of(place * half, half), half)]


def first_kernel(place_ref, keys_ref, targets_ref, rate_ref, w_ref, wb_ref, *outs):
    wb_ref[...] = w_ref[...].astype(bf16)
    grads(place_ref[0], keys_ref, targets_ref, rate_ref, wb_ref, outs[-1], outs)


def renew(starts_ref, square_ref, w_ref, pieces, new_ref, out_ref, sem, wb_ref=None):
    mean = jnp.full((1, HID), square_ref[0, 0] / float(HEADS * ROWS * HID), f32)
    factor = fast_rate / jnp.sqrt(mean + epsilon)
    rows = ROWS // 8
    copies = []
    for i in range(2 * len(pieces)):
        at = pl.ds(pl.multiple_of(starts_ref[i], rows), rows)
        new = w_ref[at] - factor * pieces[i // 2][i % 2 * rows : (i % 2 + 1) * rows].astype(f32)
        new_ref[at] = new
        copies.append(pltpu.make_async_copy(new_ref.at[at], out_ref.at[at], sem.at[i]))
        copies[-1].start()
        if wb_ref is not None:
            wb_ref[at] = new.astype(bf16)
    return copies


def second_kernel(place_ref, starts_ref, square_ref, keys_ref, targets_ref, rate_ref, w_ref, *rest):
    pieces, (out_ref, wb_ref, *outs, grad_ref, new_ref, sem) = rest[:4], rest[4:]
    copies = renew(starts_ref, square_ref, w_ref, pieces, new_ref, out_ref, sem, wb_ref)
    grads(place_ref[0], keys_ref, targets_ref, rate_ref, wb_ref, grad_ref, outs)
    for copy in copies:
        copy.wait()


def last_kernel(starts_ref, square_ref, w_ref, *rest):
    pieces, (out_ref, new_ref, sem) = rest[:4], rest[4:]
    for copy in renew(starts_ref, square_ref, w_ref, pieces, new_ref, out_ref, sem):
        copy.wait()


def attend_kernel(meta_ref, q_ref, halo_ref, k_ref, v_ref, out_ref):
    local = q_ref.shape[0]
    anchor, width = meta_ref[0], meta_ref[1]
    scale = HD ** (-0.5)
    held = [(halo_ref, halo_ref.at[WIN:], -WIN, WIN), (k_ref, v_ref, 0, local)]
    for start in range(0, local, TILE):
        spans = []
        for keys, values, base, count in held:
            low, high = max(base, start - WIN), min(base + count, start + TILE)
            if low < high:
                spans.append((keys, values, low - base, high - base, low))
        query = q_ref[start : start + TILE]
        scores = []
        for keys, _, low, high, position in spans:
            s = dot(query, keys[low:high], 1, 1) * scale
            row = lax.broadcasted_iota(jnp.int32, s.shape, 0) + start
            col = lax.broadcasted_iota(jnp.int32, s.shape, 1) + position
            live = (col <= row) & (col > row - width) & (col >= -anchor)
            scores.append(jnp.where(live, s, -1e30))
        peak = functools.reduce(jnp.maximum, [jnp.max(s, axis=1, keepdims=True) for s in scores])
        expo = [jnp.exp(s - peak) for s in scores]
        total = sum(jnp.sum(e, axis=1, keepdims=True) for e in expo)
        inverse = 1.0 / total
        attn = 0.0
        for e, (_, values, low, high, _) in zip(expo, spans):
            attn = attn + dot((e * inverse).astype(bf16), values[low:high], 1, 0)
        out_ref[start : start + TILE] = attn


def apply_kernel(meta_ref, q_ref, attn_ref, early_ref, late_ref, out_ref, y_ref):
    anchor, split = meta_ref[0], meta_ref[2]

    def fast(query, wb_ref):
        first = dot(query, wb_ref[0:HD], 1, 0)
        third = dot(query, wb_ref[HD : 2 * HD], 1, 0)
        act = (first * jax.nn.sigmoid(first) * third).astype(bf16)
        return dot(act, wb_ref[2 * HD :], 1, 1)

    def tile(i, carry):
        start = pl.multiple_of(i * TILE, TILE)
        rows = pl.ds(start, TILE)

        @pl.when(anchor + start < split)
        def _():
            y_ref[...] = fast(q_ref[rows], early_ref)

        @pl.when(anchor + start + TILE > split)
        def _():
            late = fast(q_ref[rows], late_ref)
            position = anchor + start + lax.broadcasted_iota(jnp.int32, late.shape, 0)
            y_ref[...] = jnp.where(position < split, y_ref[...], late)

        y = y_ref[...]
        norm = y / jnp.sqrt(jnp.mean(y * y, axis=1, keepdims=True) + epsilon)
        out_ref[rows] = (attn_ref[rows] + norm).astype(bf16)
        return carry

    lax.fori_loop(0, q_ref.shape[0] // TILE, tile, 0)


def call(kernel, specs, outs, args, megabytes, scratch=(), out_specs=None):
    return pl.pallas_call(
        kernel,
        out_shape=outs,
        in_specs=specs,
        out_specs=jax.tree.map(lambda _: VMEM_SPEC, outs) if out_specs is None else out_specs,
        scratch_shapes=list(scratch),
        compiler_params=pltpu.CompilerParams(vmem_limit_bytes=megabytes << 20),
    )(*args)


def array(shape, dtype):
    return jax.ShapeDtypeStruct(shape, dtype)


def per_device(queries, keys, values, targets, token_rate, window, split, fast_init):
    local = queries.shape[0]
    anchor = lax.axis_index(SEQ) * local
    count = lax.axis_size(SEQ)
    onward = [(i, i + 1) for i in range(count - 1)]
    tail = jnp.concatenate([keys[local - WIN :], values[local - WIN :]], axis=0)
    halo = lax.ppermute(tail, SEQ, onward)
    positions = anchor + jnp.arange(local, dtype=jnp.int32)[:, None]
    first_block = (positions < split[0]).astype(f32)
    rate_zero = token_rate * first_block
    rate_one = token_rate * (1.0 - first_block)
    core = lax.axis_index("core").astype(jnp.int32).reshape(1)
    starts = piece_starts()
    meta = jnp.stack([anchor, window[0], split[0]]).astype(jnp.int32)
    weights_zero = fast_init.reshape(ROWS, HID)
    half = ROWS // 2
    wide = [array((half, HID // CHUNKS), kind) for kind in (bf16, f32) for _ in range(CHUNKS)]
    grad = pltpu.VMEM((ROWS, HID // CHUNKS), f32)
    renewal = [pltpu.VMEM((ROWS, HID), f32), pltpu.SemaphoreType.DMA((8,))]

    wb_zero, *halved = call(
        first_kernel,
        [SMEM_SPEC] + [VMEM_SPEC] * 4,
        [array((ROWS, HID), bf16)] + wide,
        (core, keys, targets, rate_zero, weights_zero),
        28,
        [grad],
    )

    def finished(mine, other):
        total, square = call(
            finish_kernel,
            [VMEM_SPEC] * (2 * CHUNKS),
            [array((ROWS // 8, HID), bf16), array((8, 128), f32)],
            (*mine, *other),
            8,
        )
        return over_seq_and_head(square), gathered(total)

    square, pieces = finished(*reduced(halved[:CHUNKS], halved[CHUNKS:]))
    weights_one, wb_one, *halved = call(
        second_kernel,
        [SMEM_SPEC] * 3 + [VMEM_SPEC] * 8,
        [array((ROWS, HID), f32), array((ROWS, HID), bf16)] + wide,
        (core, starts, square, keys, targets, rate_one, weights_zero, *pieces),
        32,
        [grad] + renewal,
        [ANY_SPEC] + [VMEM_SPEC] * (1 + 2 * CHUNKS),
    )
    kept = {}

    def attend(before, after):
        query, _ = lax.optimization_barrier((queries, before))
        attn = call(
            attend_kernel,
            [SMEM_SPEC] + [VMEM_SPEC] * 4,
            array((local, HD), f32),
            (meta, query, halo, keys, values),
            20,
        )
        kept["attn"], after = lax.optimization_barrier((attn, after))
        return after

    def apply(before, after):
        query, _ = lax.optimization_barrier((queries, before))
        outputs = call(
            apply_kernel,
            [SMEM_SPEC] + [VMEM_SPEC] * 4,
            array((local, HD), bf16),
            (meta, query, kept["attn"], wb_zero, wb_one),
            20,
            [pltpu.VMEM((TILE, HD), f32)],
        )
        kept["outputs"], after = lax.optimization_barrier((outputs, after))
        return after

    square, pieces = finished(*reduced(halved[:CHUNKS], halved[CHUNKS:], attend, apply))
    weights_two = call(
        last_kernel,
        [SMEM_SPEC] * 2 + [VMEM_SPEC] * 5,
        array((ROWS, HID), f32),
        (starts, square, weights_one, *pieces),
        20,
        renewal,
        ANY_SPEC,
    )
    return (kept["outputs"], weights_two.reshape(1, 3, HD, HID))


def solution(mesh):
    finer = Mesh(mesh.devices.reshape(4, 4, 2, mesh.shape["head"]), ("z", "x", "core", "head"))
    tokens = P(SEQ, "head")
    weights = P("head", None, None, None)
    return jax.shard_map(
        per_device,
        mesh=finer,
        in_specs=(tokens,) * 5 + (P("head"), P(), weights),
        out_specs=(tokens, weights),
        check_vma=False,
    )
```

```python
import functools
import math

import jax
import jax.numpy as jnp
from jax import lax
from jax.experimental import pallas as pl
from jax.experimental.pallas import tpu as pltpu
from jax.sharding import Mesh
from jax.sharding import PartitionSpec as P

HEADS = 8
HD = 512
HID = 512
WIN = 512
ROWS = 3 * HD
SEQ = ("z", "x", "core")
TILE = 256
CHUNKS = 2
SHARES = 64

fast_rate = 0.01
epsilon = 1e-06
bf16 = jnp.bfloat16
f32 = jnp.float32
VMEM_SPEC = pl.BlockSpec(memory_space=pltpu.VMEM)
SMEM_SPEC = pl.BlockSpec(memory_space=pltpu.SMEM)
ANY_SPEC = pl.BlockSpec(memory_space=pl.ANY)
HBM_SPEC = pl.BlockSpec(memory_space=pltpu.HBM)


def dot(a, b, over_a, over_b):
    return lax.dot_general(a, b, (((over_a,), (over_b,)), ((), ())), preferred_element_type=f32)


def exchange(value, mesh_axes, partner):
    count = math.prod(lax.axis_size(a) for a in mesh_axes)
    return lax.ppermute(value, mesh_axes, [(i, partner(i)) for i in range(count)])


def ring_pair(step):
    def partner(i):
        place, core = divmod(i, 2)
        return (place ^ (1 if core == step else 3)) * 2 + core

    return partner


def swap_x(value, step):
    return exchange(value, ("x", "core"), ring_pair(step))


def swap_z(value, step):
    return exchange(value, ("z", "core"), ring_pair(step))


def swap_core(value):
    return exchange(value, ("core",), lambda i: i ^ 1)


def spread(squares):
    return lax.all_to_all(squares, ("x", "core", "head"), 0, 0, tiled=True)


def rows_of(value, start, count):
    return lax.dynamic_slice_in_dim(value, start, count, 0)


def halves():
    core = lax.axis_index("core")
    place = lax.axis_index("x")
    low, high = place & 1, place >> 1
    first = jnp.where(core == 0, low ^ high, high)
    second = jnp.where(core == 0, high, low ^ high)
    return core, first, second


def piece_starts():
    core, a, b = halves()
    here = [(a, b), (a, 1 - b), (1 - a, b), (1 - a, 1 - b)]
    there = [(b, a), (b, 1 - a), (1 - b, a), (1 - b, 1 - a)]
    places = [core * 4 + i * 2 + j for i, j in here] + [(1 - core) * 4 + i * 2 + j for i, j in there]
    return (jnp.stack(places) * (ROWS // 8)).astype(jnp.int32)


def reduced(sent, own, before_z=None, beside_first=None, beside_second=None):
    _, first, second = halves()
    half, rows = ROWS // 4, ROWS // 8
    chunks = range(len(sent))
    got = [swap_core(s) for s in sent]

    def two(c, start, count):
        return rows_of(own[c], start, count) + rows_of(got[c], start, count).astype(f32)

    got_x = [swap_x(two(c, (1 - first) * half, half).astype(bf16), 0) for c in chunks]
    away = (1 - second) * rows
    send = [(two(c, first * half + away, rows) + rows_of(got_x[c], away, rows).astype(f32)).astype(bf16) for c in chunks]
    got_x2 = [swap_x(s, 1) for s in send]
    near = second * rows
    mine = [two(c, first * half + near, rows) + rows_of(got_x[c], near, rows).astype(f32) + got_x2[c].astype(f32) for c in chunks]
    mine = [m.astype(bf16) for m in mine]
    if before_z is not None:
        mine = before_z(mine)
    other = [swap_z(m, 0) for m in mine]
    if beside_first is not None:
        other = beside_first(mine, other)
    mine = [(m.astype(f32) + o.astype(f32)).astype(bf16) for m, o in zip(mine, other)]
    other = [swap_z(m, 1) for m in mine]
    if beside_second is not None:
        other = beside_second(mine, other)
    return mine, other


def gathered(own):
    near = swap_x(own, 1)
    pair = jnp.concatenate([own, near], axis=0)
    far = swap_x(pair, 0)
    return [pair, far, swap_core(pair), swap_core(far)]


def finish_kernel(*refs):
    total_ref, square_ref = refs[2 * CHUNKS :]
    wide = HID // CHUNKS
    for c in range(CHUNKS):
        total = refs[c][...].astype(f32) + refs[CHUNKS + c][...].astype(f32)
        total_ref[:, c * wide : (c + 1) * wide] = total.astype(bf16)
        square = jnp.sum(total * total, axis=0, keepdims=True)
        square = square if c == 0 else before + square
        before = square
    square_ref[...] = jnp.broadcast_to(jnp.sum(square, axis=1, keepdims=True), (8, 128))[None] + jnp.zeros(square_ref.shape, f32)


def fetch(sources, targets, sem):
    copies = [pltpu.make_async_copy(a, b, sem.at[i]) for i, (a, b) in enumerate(zip(sources, targets))]
    for copy in copies:
        copy.start()
    return copies


def grads(place, keys_ref, targets_ref, rate_ref, wb_ref, grad_ref, outs):
    keys = keys_ref[...]
    d_out = (-rate_ref[...] * targets_ref[...].astype(f32)).astype(bf16)
    half, wide = ROWS // 2, HID // CHUNKS
    for c in range(CHUNKS):
        cols = slice(c * wide, (c + 1) * wide)
        first = dot(keys, wb_ref[0:HD, cols], 1, 0)
        third = dot(keys, wb_ref[HD : 2 * HD, cols], 1, 0)
        d_act = dot(d_out, wb_ref[2 * HD :, cols], 1, 0)
        sigma = jax.nn.sigmoid(first)
        swish = first * sigma
        act = (swish * third).astype(bf16)
        d_first = (d_act * third * sigma * (1.0 + first * (1.0 - sigma))).astype(bf16)
        d_third = (d_act * swish).astype(bf16)
        grad_ref[0:HD] = dot(keys, d_first, 0, 0)
        grad_ref[HD : 2 * HD] = dot(keys, d_third, 0, 0)
        grad_ref[2 * HD :] = dot(d_out, act, 0, 0)
        outs[c][...] = grad_ref[pl.ds(pl.multiple_of((1 - place) * half, half), half)].astype(bf16)
        outs[CHUNKS + c][...] = grad_ref[pl.ds(pl.multiple_of(place * half, half), half)]


def first_kernel(place_ref, keys_hbm, targets_hbm, rate_ref, w_hbm, wb_hbm, *rest):
    outs, (grad_ref, keys_ref, targets_ref, w_ref, wb_ref, sem) = rest[: 2 * CHUNKS], rest[2 * CHUNKS :]
    thirds = [pl.ds(i * HD, HD) for i in range(3)]
    copies = fetch(
        [w_hbm.at[t] for t in thirds] + [keys_hbm, targets_hbm],
        [w_ref.at[t] for t in thirds] + [keys_ref, targets_ref],
        sem,
    )
    for copy, third in zip(copies, thirds):
        copy.wait()
        wb_ref[third] = w_ref[third].astype(bf16)
    leave = pltpu.make_async_copy(wb_ref, wb_hbm, sem.at[5])
    leave.start()
    copies[3].wait()
    copies[4].wait()
    grads(place_ref[0], keys_ref, targets_ref, rate_ref, wb_ref, grad_ref, outs)
    leave.wait()


def piece_rows(starts_ref):
    rows = ROWS // 8
    return [pl.ds(pl.multiple_of(starts_ref[i], rows), rows) for i in range(8)]


def renew(starts_ref, square_ref, w_ref, pieces, new_ref, out_ref, sem, wb_ref=None, arrive=None):
    mean = jnp.sum(square_ref[...], axis=0)[0:1, 0:1] / float(HEADS * ROWS * HID)
    factor = fast_rate / jnp.sqrt(mean + epsilon)
    rows = ROWS // 8
    copies = []
    for i, at in enumerate(piece_rows(starts_ref)):
        if arrive is not None:
            arrive[i].wait()
        new = w_ref[at] - factor * pieces[i // 2][i % 2 * rows : (i % 2 + 1) * rows].astype(f32)
        new_ref[at] = new
        copies.append(pltpu.make_async_copy(new_ref.at[at], out_ref.at[at], sem.at[i]))
        copies[-1].start()
        if wb_ref is not None:
            wb_ref[at] = new.astype(bf16)
    return copies


def second_kernel(place_ref, starts_ref, square_ref, keys_hbm, targets_hbm, rate_ref, w_hbm, *rest):
    pieces, (out_ref, wb_ref, *outs) = rest[:4], rest[4 : 6 + 2 * CHUNKS]
    grad_ref, new_ref, sem, keys_ref, targets_ref, w_ref, fetched = rest[6 + 2 * CHUNKS :]
    spans = piece_rows(starts_ref)
    arrive = fetch(
        [w_hbm.at[at] for at in spans] + [keys_hbm, targets_hbm],
        [w_ref.at[at] for at in spans] + [keys_ref, targets_ref],
        fetched,
    )
    copies = renew(starts_ref, square_ref, w_ref, pieces, new_ref, out_ref, sem, wb_ref, arrive)
    for copy in arrive[8:]:
        copy.wait()
    grads(place_ref[0], keys_ref, targets_ref, rate_ref, wb_ref, grad_ref, outs)
    for copy in copies:
        copy.wait()


def last_kernel(starts_ref, square_ref, w_ref, *rest):
    pieces, (out_ref, new_ref, sem) = rest[:4], rest[4:]
    for copy in renew(starts_ref, square_ref, w_ref, pieces, new_ref, out_ref, sem):
        copy.wait()


def attend_kernel(meta_ref, q_ref, halo_k_ref, k_ref, halo_v_ref, v_ref, out_ref):
    local = q_ref.shape[0]
    anchor, width = meta_ref[0], meta_ref[1]
    scale = HD ** (-0.5)
    held = [(halo_k_ref, halo_v_ref, -WIN, WIN), (k_ref, v_ref, 0, local)]
    for start in range(0, local, TILE):
        spans = []
        for keys, values, base, count in held:
            low, high = max(base, start - WIN), min(base + count, start + TILE)
            if low < high:
                spans.append((keys, values, low - base, high - base, low))
        query = q_ref[start : start + TILE]
        scores = []
        for keys, _, low, high, position in spans:
            s = dot(query, keys[low:high], 1, 1) * scale
            row = lax.broadcasted_iota(jnp.int32, s.shape, 0) + start
            col = lax.broadcasted_iota(jnp.int32, s.shape, 1) + position
            live = (col <= row) & (col > row - width) & (col >= -anchor)
            scores.append(jnp.where(live, s, -1e30))
        peak = functools.reduce(jnp.maximum, [jnp.max(s, axis=1, keepdims=True) for s in scores])
        expo = [jnp.exp(s - peak) for s in scores]
        total = sum(jnp.sum(e, axis=1, keepdims=True) for e in expo)
        inverse = 1.0 / total
        attn = 0.0
        for e, (_, values, low, high, _) in zip(expo, spans):
            attn = attn + dot((e * inverse).astype(bf16), values[low:high], 1, 0)
        out_ref[start : start + TILE] = attn


def apply_kernel(meta_ref, q_ref, attn_ref, early_ref, late_ref, out_ref, y_ref):
    anchor, split = meta_ref[0], meta_ref[2]

    def fast(query, wb_ref):
        first = dot(query, wb_ref[0:HD], 1, 0)
        third = dot(query, wb_ref[HD : 2 * HD], 1, 0)
        act = (first * jax.nn.sigmoid(first) * third).astype(bf16)
        return dot(act, wb_ref[2 * HD :], 1, 1)

    def tile(i, carry):
        start = pl.multiple_of(i * TILE, TILE)
        rows = pl.ds(start, TILE)

        @pl.when(anchor + start < split)
        def _():
            y_ref[...] = fast(q_ref[rows], early_ref)

        @pl.when(anchor + start + TILE > split)
        def _():
            late = fast(q_ref[rows], late_ref)
            position = anchor + start + lax.broadcasted_iota(jnp.int32, late.shape, 0)
            y_ref[...] = jnp.where(position < split, y_ref[...], late)

        y = y_ref[...]
        norm = y / jnp.sqrt(jnp.mean(y * y, axis=1, keepdims=True) + epsilon)
        out_ref[rows] = (attn_ref[rows] + norm).astype(bf16)
        return carry

    lax.fori_loop(0, q_ref.shape[0] // TILE, tile, 0)


def call(kernel, specs, outs, args, megabytes, scratch=(), out_specs=None):
    return pl.pallas_call(
        kernel,
        out_shape=outs,
        in_specs=specs,
        out_specs=jax.tree.map(lambda _: VMEM_SPEC, outs) if out_specs is None else out_specs,
        scratch_shapes=list(scratch),
        compiler_params=pltpu.CompilerParams(vmem_limit_bytes=megabytes << 20),
    )(*args)


def in_hbm(value):
    return pltpu.with_memory_space_constraint(value, pltpu.HBM)


def array(shape, dtype):
    return jax.ShapeDtypeStruct(shape, dtype)


def per_device(queries, keys, values, targets, token_rate, window, split, fast_init):
    local = queries.shape[0]
    anchor = lax.axis_index(SEQ) * local
    count = lax.axis_size(SEQ)
    onward = [(i, i + 1) for i in range(count - 1)]
    halo_k = lax.ppermute(keys[local - WIN :], SEQ, onward)
    halo_v = lax.ppermute(values[local - WIN :], SEQ, onward)
    positions = anchor + jnp.arange(local, dtype=jnp.int32)[:, None]
    first_block = (positions < split[0]).astype(f32)
    rate_zero = token_rate * first_block
    rate_one = token_rate * (1.0 - first_block)
    core = lax.axis_index("core").astype(jnp.int32).reshape(1)
    starts = piece_starts()
    meta = jnp.stack([anchor, window[0], split[0]]).astype(jnp.int32)
    weights_zero = fast_init.reshape(ROWS, HID)
    half = ROWS // 2
    wide = [array((half, HID // CHUNKS), kind) for kind in (bf16, f32) for _ in range(CHUNKS)]
    grad = pltpu.VMEM((ROWS, HID // CHUNKS), f32)
    renewal = [pltpu.VMEM((ROWS, HID), f32), pltpu.SemaphoreType.DMA((8,))]

    fetched = [pltpu.VMEM((local, HD), bf16)] * 2

    wb_zero, *halved = call(
        first_kernel,
        [SMEM_SPEC, HBM_SPEC, HBM_SPEC, VMEM_SPEC, HBM_SPEC],
        [pltpu.HBM((ROWS, HID), bf16)] + wide,
        (core, in_hbm(keys), in_hbm(targets), rate_zero, in_hbm(weights_zero)),
        24,
        [grad] + fetched + [pltpu.VMEM((ROWS, HID), f32), pltpu.VMEM((ROWS, HID), bf16), pltpu.SemaphoreType.DMA((6,))],
        [HBM_SPEC] + [VMEM_SPEC] * (2 * CHUNKS),
    )

    def finished(mine, other):
        total, square = call(
            finish_kernel,
            [VMEM_SPEC] * (2 * CHUNKS),
            [array((ROWS // 8, HID), bf16), array((SHARES, 8, 128), f32)],
            (*mine, *other),
            8,
        )
        return spread(square), gathered(total)

    kept = {}

    def have_keys(mine):
        kept["halo"], mine = lax.optimization_barrier((halo_k, mine))
        return mine

    square, pieces = finished(*reduced(halved[:CHUNKS], halved[CHUNKS:], have_keys))
    weights_one, wb_one, *halved = call(
        second_kernel,
        [SMEM_SPEC] * 2 + [VMEM_SPEC, HBM_SPEC, HBM_SPEC, VMEM_SPEC, HBM_SPEC] + [VMEM_SPEC] * 4,
        [pltpu.HBM((ROWS, HID), f32), array((ROWS, HID), bf16)] + wide,
        (core, starts, square, in_hbm(keys), in_hbm(targets), rate_one, in_hbm(weights_zero), *pieces),
        24,
        [grad] + renewal + fetched + [pltpu.VMEM((ROWS, HID), f32), pltpu.SemaphoreType.DMA((10,))],
        [HBM_SPEC] + [VMEM_SPEC] * (1 + 2 * CHUNKS),
    )
    def attend(before, after):
        query, _ = lax.optimization_barrier((queries, before))
        attn = call(
            attend_kernel,
            [SMEM_SPEC] + [VMEM_SPEC] * 5,
            array((local, HD), f32),
            (meta, query, kept["halo"], keys, halo_v, values),
            20,
        )
        kept["attn"], after = lax.optimization_barrier((attn, after))
        return after

    def apply(before, after):
        query, _ = lax.optimization_barrier((queries, before))
        outputs = call(
            apply_kernel,
            [SMEM_SPEC] + [VMEM_SPEC] * 4,
            array((local, HD), bf16),
            (meta, query, kept["attn"], wb_zero, wb_one),
            20,
            [pltpu.VMEM((TILE, HD), f32)],
        )
        kept["outputs"], after = lax.optimization_barrier((outputs, after))
        return after

    square, pieces = finished(*reduced(halved[:CHUNKS], halved[CHUNKS:], None, attend, apply))
    weights_two = call(
        last_kernel,
        [SMEM_SPEC] + [VMEM_SPEC] * 6,
        array((ROWS, HID), f32),
        (starts, square, weights_one, *pieces),
        20,
        renewal,
        ANY_SPEC,
    )
    return (kept["outputs"], weights_two.reshape(1, 3, HD, HID))


def solution(mesh):
    finer = Mesh(mesh.devices.reshape(4, 4, 2, mesh.shape["head"]), ("z", "x", "core", "head"))
    tokens = P(SEQ, "head")
    weights = P("head", None, None, None)
    return jax.shard_map(
        per_device,
        mesh=finer,
        in_specs=(tokens,) * 5 + (P("head"), P(), weights),
        out_specs=(tokens, weights),
        check_vma=False,
    )
```

```python
import functools
import math

import jax
import jax.numpy as jnp
from jax import lax
from jax.experimental import pallas as pl
from jax.experimental.pallas import tpu as pltpu
from jax.sharding import Mesh
from jax.sharding import PartitionSpec as P

HEADS = 8
HD = 512
HID = 512
WIN = 512
ROWS = 3 * HD
SEQ = ("z", "x", "core")
TILE = 256
CHUNKS = 2
SHARES = 64
EARLY = 128

fast_rate = 0.01
epsilon = 1e-06
bf16 = jnp.bfloat16
f32 = jnp.float32
VMEM_SPEC = pl.BlockSpec(memory_space=pltpu.VMEM)
SMEM_SPEC = pl.BlockSpec(memory_space=pltpu.SMEM)
ANY_SPEC = pl.BlockSpec(memory_space=pl.ANY)
HBM_SPEC = pl.BlockSpec(memory_space=pltpu.HBM)


def dot(a, b, over_a, over_b):
    return lax.dot_general(a, b, (((over_a,), (over_b,)), ((), ())), preferred_element_type=f32)


def exchange(value, mesh_axes, partner):
    count = math.prod(lax.axis_size(a) for a in mesh_axes)
    return lax.ppermute(value, mesh_axes, [(i, partner(i)) for i in range(count)])


def ring_pair(step):
    def partner(i):
        place, core = divmod(i, 2)
        return (place ^ (1 if core == step else 3)) * 2 + core

    return partner


def swap_x(value, step):
    return exchange(value, ("x", "core"), ring_pair(step))


def swap_z(value, step):
    return exchange(value, ("z", "core"), ring_pair(step))


def swap_core(value):
    return exchange(value, ("core",), lambda i: i ^ 1)


def chained(parts, send):
    arrived = []
    for value in parts:
        if arrived:
            value, arrived[-1] = lax.optimization_barrier((value, arrived[-1]))
        arrived.append(send(value))
    return arrived


def spread(squares):
    return lax.all_to_all(squares, ("x", "core", "head"), 0, 0, tiled=True)


def rows_of(value, start, count):
    return lax.dynamic_slice_in_dim(value, start, count, 0)


def halves():
    core = lax.axis_index("core")
    place = lax.axis_index("x")
    low, high = place & 1, place >> 1
    first = jnp.where(core == 0, low ^ high, high)
    second = jnp.where(core == 0, high, low ^ high)
    return core, first, second


def piece_starts():
    core, a, b = halves()
    here = [(a, b), (a, 1 - b), (1 - a, b), (1 - a, 1 - b)]
    there = [(b, a), (b, 1 - a), (1 - b, a), (1 - b, 1 - a)]
    places = [core * 4 + i * 2 + j for i, j in here] + [(1 - core) * 4 + i * 2 + j for i, j in there]
    return (jnp.stack(places) * (ROWS // 8)).astype(jnp.int32)


def reduced(sent, own, beside_first=None, beside_second=None):
    _, first, second = halves()
    half, rows = ROWS // 4, ROWS // 8
    chunks = range(len(sent))
    got = [swap_core(s) for s in sent]

    def two(c, start, count):
        return rows_of(own[c], start, count) + rows_of(got[c], start, count).astype(f32)

    got_x = [swap_x(two(c, (1 - first) * half, half).astype(bf16), 0) for c in chunks]
    away = (1 - second) * rows
    send = [(two(c, first * half + away, rows) + rows_of(got_x[c], away, rows).astype(f32)).astype(bf16) for c in chunks]
    got_x2 = [swap_x(s, 1) for s in send]
    near = second * rows
    mine = [two(c, first * half + near, rows) + rows_of(got_x[c], near, rows).astype(f32) + got_x2[c].astype(f32) for c in chunks]
    mine = [m.astype(bf16) for m in mine]
    other = [swap_z(m, 0) for m in mine]
    if beside_first is not None:
        other = beside_first(mine, other)
    mine = [(m.astype(f32) + o.astype(f32)).astype(bf16) for m, o in zip(mine, other)]
    other = [swap_z(m, 1) for m in mine]
    if beside_second is not None:
        other = beside_second(mine, other)
    return mine, other


def gathered(own):
    near = swap_x(own, 1)
    pair = jnp.concatenate([own, near], axis=0)
    far = swap_x(pair, 0)
    return [pair, far, swap_core(pair), swap_core(far)]


def finish_kernel(*refs):
    total_ref, square_ref = refs[2 * CHUNKS :]
    wide = HID // CHUNKS
    for c in range(CHUNKS):
        total = refs[c][...].astype(f32) + refs[CHUNKS + c][...].astype(f32)
        total_ref[:, c * wide : (c + 1) * wide] = total.astype(bf16)
        square = jnp.sum(total * total, axis=0, keepdims=True)
        square = square if c == 0 else before + square
        before = square
    square_ref[...] = jnp.broadcast_to(jnp.sum(square, axis=1, keepdims=True), (8, 128))[None] + jnp.zeros(square_ref.shape, f32)


def fetch(sources, targets, sem):
    copies = [pltpu.make_async_copy(a, b, sem.at[i]) for i, (a, b) in enumerate(zip(sources, targets))]
    for copy in copies:
        copy.start()
    return copies


def grads(place, keys_ref, targets_ref, rate_ref, wb_ref, grad_ref, outs):
    keys = keys_ref[...]
    d_out = (-rate_ref[...] * targets_ref[...].astype(f32)).astype(bf16)
    half, wide = ROWS // 2, HID // CHUNKS
    for c in range(CHUNKS):
        cols = slice(c * wide, (c + 1) * wide)
        first = dot(keys, wb_ref[0:HD, cols], 1, 0)
        third = dot(keys, wb_ref[HD : 2 * HD, cols], 1, 0)
        d_act = dot(d_out, wb_ref[2 * HD :, cols], 1, 0)
        sigma = jax.nn.sigmoid(first)
        swish = first * sigma
        act = (swish * third).astype(bf16)
        d_first = (d_act * third * sigma * (1.0 + first * (1.0 - sigma))).astype(bf16)
        d_third = (d_act * swish).astype(bf16)
        grad_ref[0:HD] = dot(keys, d_first, 0, 0)
        grad_ref[HD : 2 * HD] = dot(keys, d_third, 0, 0)
        grad_ref[2 * HD :] = dot(d_out, act, 0, 0)
        outs[c][...] = grad_ref[pl.ds(pl.multiple_of((1 - place) * half, half), half)].astype(bf16)
        outs[CHUNKS + c][...] = grad_ref[pl.ds(pl.multiple_of(place * half, half), half)]


def first_kernel(place_ref, keys_hbm, targets_hbm, rate_ref, w_hbm, wb_hbm, *rest):
    outs, (grad_ref, keys_ref, targets_ref, w_ref, wb_ref, sem) = rest[: 2 * CHUNKS], rest[2 * CHUNKS :]
    thirds = [pl.ds(i * HD, HD) for i in range(3)]
    copies = fetch(
        [w_hbm.at[t] for t in thirds] + [keys_hbm, targets_hbm],
        [w_ref.at[t] for t in thirds] + [keys_ref, targets_ref],
        sem,
    )
    for copy, third in zip(copies, thirds):
        copy.wait()
        wb_ref[third] = w_ref[third].astype(bf16)
    leave = pltpu.make_async_copy(wb_ref, wb_hbm, sem.at[5])
    leave.start()
    copies[3].wait()
    copies[4].wait()
    grads(place_ref[0], keys_ref, targets_ref, rate_ref, wb_ref, grad_ref, outs)
    leave.wait()


def piece_rows(starts_ref):
    rows = ROWS // 8
    return [pl.ds(pl.multiple_of(starts_ref[i], rows), rows) for i in range(8)]


def renew(starts_ref, square_ref, w_ref, pieces, new_ref, out_ref, sem, wb_ref=None, arrive=None):
    mean = jnp.sum(square_ref[...], axis=0)[0:1, 0:1] / float(HEADS * ROWS * HID)
    factor = fast_rate / jnp.sqrt(mean + epsilon)
    rows = ROWS // 8
    copies = []
    for i, at in enumerate(piece_rows(starts_ref)):
        if arrive is not None:
            arrive[i].wait()
        new = w_ref[at] - factor * pieces[i // 2][i % 2 * rows : (i % 2 + 1) * rows].astype(f32)
        new_ref[at] = new
        copies.append(pltpu.make_async_copy(new_ref.at[at], out_ref.at[at], sem.at[i]))
        copies[-1].start()
        if wb_ref is not None:
            wb_ref[at] = new.astype(bf16)
    return copies


def second_kernel(place_ref, starts_ref, square_ref, keys_hbm, targets_hbm, rate_ref, w_hbm, *rest):
    pieces, (out_ref, wb_ref, *outs) = rest[:4], rest[4 : 6 + 2 * CHUNKS]
    grad_ref, new_ref, sem, keys_ref, targets_ref, w_ref, fetched = rest[6 + 2 * CHUNKS :]
    spans = piece_rows(starts_ref)
    arrive = fetch(
        [w_hbm.at[at] for at in spans] + [keys_hbm, targets_hbm],
        [w_ref.at[at] for at in spans] + [keys_ref, targets_ref],
        fetched,
    )
    copies = renew(starts_ref, square_ref, w_ref, pieces, new_ref, out_ref, sem, wb_ref, arrive)
    for copy in arrive[8:]:
        copy.wait()
    grads(place_ref[0], keys_ref, targets_ref, rate_ref, wb_ref, grad_ref, outs)
    for copy in copies:
        copy.wait()


def last_kernel(starts_ref, square_ref, w_ref, *rest):
    pieces, (out_ref, new_ref, sem) = rest[:4], rest[4:]
    for copy in renew(starts_ref, square_ref, w_ref, pieces, new_ref, out_ref, sem):
        copy.wait()


def attend_kernel(meta_ref, q_ref, halo_k_ref, k_ref, halo_v0, halo_v1, v_ref, out_ref, halo_v_ref):
    local = q_ref.shape[0]
    anchor, width = meta_ref[0], meta_ref[1]
    scale = HD ** (-0.5)
    halo_v_ref[0:EARLY] = halo_v0[...]
    halo_v_ref[EARLY:] = halo_v1[...]
    held = [(halo_k_ref, halo_v_ref, -WIN, WIN), (k_ref, v_ref, 0, local)]
    for start in range(0, local, TILE):
        spans = []
        for keys, values, base, count in held:
            low, high = max(base, start - WIN), min(base + count, start + TILE)
            if low < high:
                spans.append((keys, values, low - base, high - base, low))
        query = q_ref[start : start + TILE]
        scores = []
        for keys, _, low, high, position in spans:
            s = dot(query, keys[low:high], 1, 1) * scale
            row = lax.broadcasted_iota(jnp.int32, s.shape, 0) + start
            col = lax.broadcasted_iota(jnp.int32, s.shape, 1) + position
            live = (col <= row) & (col > row - width) & (col >= -anchor)
            scores.append(jnp.where(live, s, -1e30))
        peak = functools.reduce(jnp.maximum, [jnp.max(s, axis=1, keepdims=True) for s in scores])
        expo = [jnp.exp(s - peak) for s in scores]
        total = sum(jnp.sum(e, axis=1, keepdims=True) for e in expo)
        inverse = 1.0 / total
        attn = 0.0
        for e, (_, values, low, high, _) in zip(expo, spans):
            attn = attn + dot((e * inverse).astype(bf16), values[low:high], 1, 0)
        out_ref[start : start + TILE] = attn


def apply_kernel(meta_ref, q_ref, attn_ref, early_ref, late_ref, out_ref, y_ref):
    anchor, split = meta_ref[0], meta_ref[2]

    def fast(query, wb_ref):
        first = dot(query, wb_ref[0:HD], 1, 0)
        third = dot(query, wb_ref[HD : 2 * HD], 1, 0)
        act = (first * jax.nn.sigmoid(first) * third).astype(bf16)
        return dot(act, wb_ref[2 * HD :], 1, 1)

    def tile(i, carry):
        start = pl.multiple_of(i * TILE, TILE)
        rows = pl.ds(start, TILE)

        @pl.when(anchor + start < split)
        def _():
            y_ref[...] = fast(q_ref[rows], early_ref)

        @pl.when(anchor + start + TILE > split)
        def _():
            late = fast(q_ref[rows], late_ref)
            position = anchor + start + lax.broadcasted_iota(jnp.int32, late.shape, 0)
            y_ref[...] = jnp.where(position < split, y_ref[...], late)

        y = y_ref[...]
        norm = y / jnp.sqrt(jnp.mean(y * y, axis=1, keepdims=True) + epsilon)
        out_ref[rows] = (attn_ref[rows] + norm).astype(bf16)
        return carry

    lax.fori_loop(0, q_ref.shape[0] // TILE, tile, 0)


def call(kernel, specs, outs, args, megabytes, scratch=(), out_specs=None):
    return pl.pallas_call(
        kernel,
        out_shape=outs,
        in_specs=specs,
        out_specs=jax.tree.map(lambda _: VMEM_SPEC, outs) if out_specs is None else out_specs,
        scratch_shapes=list(scratch),
        compiler_params=pltpu.CompilerParams(vmem_limit_bytes=megabytes << 20),
    )(*args)


def in_hbm(value):
    return pltpu.with_memory_space_constraint(value, pltpu.HBM)


def array(shape, dtype):
    return jax.ShapeDtypeStruct(shape, dtype)


def per_device(queries, keys, values, targets, token_rate, window, split, fast_init):
    local = queries.shape[0]
    anchor = lax.axis_index(SEQ) * local
    count = lax.axis_size(SEQ)
    onward = [(i, i + 1) for i in range(count - 1)]
    tail = local - WIN
    halo_v = chained([values[tail : tail + EARLY], values[tail + EARLY :]], lambda v: lax.ppermute(v, SEQ, onward))
    positions = anchor + jnp.arange(local, dtype=jnp.int32)[:, None]
    first_block = (positions < split[0]).astype(f32)
    rate_zero = token_rate * first_block
    rate_one = token_rate * (1.0 - first_block)
    core = lax.axis_index("core").astype(jnp.int32).reshape(1)
    starts = piece_starts()
    meta = jnp.stack([anchor, window[0], split[0]]).astype(jnp.int32)
    weights_zero = fast_init.reshape(ROWS, HID)
    half = ROWS // 2
    wide = [array((half, HID // CHUNKS), kind) for kind in (bf16, f32) for _ in range(CHUNKS)]
    grad = pltpu.VMEM((ROWS, HID // CHUNKS), f32)
    renewal = [pltpu.VMEM((ROWS, HID), f32), pltpu.SemaphoreType.DMA((8,))]

    fetched = [pltpu.VMEM((local, HD), bf16)] * 2

    wb_zero, *halved = call(
        first_kernel,
        [SMEM_SPEC, HBM_SPEC, HBM_SPEC, VMEM_SPEC, HBM_SPEC],
        [pltpu.HBM((ROWS, HID), bf16)] + wide,
        (core, in_hbm(keys), in_hbm(targets), rate_zero, in_hbm(weights_zero)),
        24,
        [grad] + fetched + [pltpu.VMEM((ROWS, HID), f32), pltpu.VMEM((ROWS, HID), bf16), pltpu.SemaphoreType.DMA((6,))],
        [HBM_SPEC] + [VMEM_SPEC] * (2 * CHUNKS),
    )

    def finished(mine, other, later):
        total, square = call(
            finish_kernel,
            [VMEM_SPEC] * (2 * CHUNKS),
            [array((ROWS // 8, HID), bf16), array((SHARES, 8, 128), f32)],
            (*mine, *other),
            8,
        )
        if later is not None:
            total, later = lax.optimization_barrier((total, later))
        return spread(square), gathered(total), later

    kept = {}

    square, pieces, send = finished(*reduced(halved[:CHUNKS], halved[CHUNKS:]), keys[tail:])
    halo_k = lax.ppermute(send, SEQ, onward)
    weights_one, wb_one, *halved = call(
        second_kernel,
        [SMEM_SPEC] * 2 + [VMEM_SPEC, HBM_SPEC, HBM_SPEC, VMEM_SPEC, HBM_SPEC] + [VMEM_SPEC] * 4,
        [pltpu.HBM((ROWS, HID), f32), array((ROWS, HID), bf16)] + wide,
        (core, starts, square, in_hbm(keys), in_hbm(targets), rate_one, in_hbm(weights_zero), *pieces),
        24,
        [grad] + renewal + fetched + [pltpu.VMEM((ROWS, HID), f32), pltpu.SemaphoreType.DMA((10,))],
        [HBM_SPEC] + [VMEM_SPEC] * (1 + 2 * CHUNKS),
    )
    kept["halo"], halved = lax.optimization_barrier((halo_k, halved))

    def attend(before, after):
        query, _ = lax.optimization_barrier((queries, before))
        attn = call(
            attend_kernel,
            [SMEM_SPEC] + [VMEM_SPEC] * 6,
            array((local, HD), f32),
            (meta, query, kept["halo"], keys, *halo_v, values),
            20,
            [pltpu.VMEM((WIN, HD), bf16)],
        )
        kept["attn"], after = lax.optimization_barrier((attn, after))
        return after

    def apply(before, after):
        query, _ = lax.optimization_barrier((queries, before))
        outputs = call(
            apply_kernel,
            [SMEM_SPEC] + [VMEM_SPEC] * 4,
            array((local, HD), bf16),
            (meta, query, kept["attn"], wb_zero, wb_one),
            20,
            [pltpu.VMEM((TILE, HD), f32)],
        )
        kept["outputs"], after = lax.optimization_barrier((outputs, after))
        return after

    square, pieces, _ = finished(*reduced(halved[:CHUNKS], halved[CHUNKS:], attend, apply), None)
    weights_two = call(
        last_kernel,
        [SMEM_SPEC] + [VMEM_SPEC] * 6,
        array((ROWS, HID), f32),
        (starts, square, weights_one, *pieces),
        20,
        renewal,
        ANY_SPEC,
    )
    return (kept["outputs"], weights_two.reshape(1, 3, HD, HID))


def solution(mesh):
    finer = Mesh(mesh.devices.reshape(4, 4, 2, mesh.shape["head"]), ("z", "x", "core", "head"))
    tokens = P(SEQ, "head")
    weights = P("head", None, None, None)
    return jax.shard_map(
        per_device,
        mesh=finer,
        in_specs=(tokens,) * 5 + (P("head"), P(), weights),
        out_specs=(tokens, weights),
        check_vma=False,
    )
```

```python
import functools
import math

import jax
import jax.numpy as jnp
from jax import lax
from jax.experimental import pallas as pl
from jax.experimental.pallas import tpu as pltpu
from jax.sharding import Mesh
from jax.sharding import PartitionSpec as P

HEADS = 8
HD = 512
HID = 512
WIN = 512
ROWS = 3 * HD
SEQ = ("z", "x", "core")
TILE = 256
CHUNKS = 2
SHARES = 64
EARLY = 256

fast_rate = 0.01
epsilon = 1e-06
bf16 = jnp.bfloat16
f32 = jnp.float32
VMEM_SPEC = pl.BlockSpec(memory_space=pltpu.VMEM)
SMEM_SPEC = pl.BlockSpec(memory_space=pltpu.SMEM)
ANY_SPEC = pl.BlockSpec(memory_space=pl.ANY)
HBM_SPEC = pl.BlockSpec(memory_space=pltpu.HBM)


def dot(a, b, over_a, over_b):
    return lax.dot_general(a, b, (((over_a,), (over_b,)), ((), ())), preferred_element_type=f32)


def exchange(value, mesh_axes, partner):
    count = math.prod(lax.axis_size(a) for a in mesh_axes)
    return lax.ppermute(value, mesh_axes, [(i, partner(i)) for i in range(count)])


def ring_pair(step):
    def partner(i):
        place, core = divmod(i, 2)
        return (place ^ (1 if core == step else 3)) * 2 + core

    return partner


def swap_x(value, step):
    return exchange(value, ("x", "core"), ring_pair(step))


def swap_z(value, step):
    return exchange(value, ("z", "core"), ring_pair(step))


def swap_core(value):
    return exchange(value, ("core",), lambda i: i ^ 1)


def spread(squares):
    return lax.all_to_all(squares, ("x", "core", "head"), 0, 0, tiled=True)


def rows_of(value, start, count):
    return lax.dynamic_slice_in_dim(value, start, count, 0)


def halves():
    core = lax.axis_index("core")
    place = lax.axis_index("x")
    low, high = place & 1, place >> 1
    first = jnp.where(core == 0, low ^ high, high)
    second = jnp.where(core == 0, high, low ^ high)
    return core, first, second


def piece_starts():
    core, a, b = halves()
    here = [(a, b), (a, 1 - b), (1 - a, b), (1 - a, 1 - b)]
    there = [(b, a), (b, 1 - a), (1 - b, a), (1 - b, 1 - a)]
    places = [core * 4 + i * 2 + j for i, j in here] + [(1 - core) * 4 + i * 2 + j for i, j in there]
    return (jnp.stack(places) * (ROWS // 8)).astype(jnp.int32)


def reduced(sent, own, beside_first=None, beside_second=None):
    _, first, second = halves()
    half, rows = ROWS // 4, ROWS // 8
    chunks = range(len(sent))
    got = [swap_core(s) for s in sent]

    def two(c, start, count):
        return rows_of(own[c], start, count) + rows_of(got[c], start, count).astype(f32)

    got_x = [swap_x(two(c, (1 - first) * half, half).astype(bf16), 0) for c in chunks]
    away = (1 - second) * rows
    send = [(two(c, first * half + away, rows) + rows_of(got_x[c], away, rows).astype(f32)).astype(bf16) for c in chunks]
    got_x2 = [swap_x(s, 1) for s in send]
    near = second * rows
    mine = [two(c, first * half + near, rows) + rows_of(got_x[c], near, rows).astype(f32) + got_x2[c].astype(f32) for c in chunks]
    mine = [m.astype(bf16) for m in mine]
    other = [swap_z(m, 0) for m in mine]
    if beside_first is not None:
        other = beside_first(mine, other)
    mine = [(m.astype(f32) + o.astype(f32)).astype(bf16) for m, o in zip(mine, other)]
    other = [swap_z(m, 1) for m in mine]
    if beside_second is not None:
        other = beside_second(mine, other)
    return mine, other


def gathered(own):
    near = swap_x(own, 1)
    pair = jnp.concatenate([own, near], axis=0)
    far = swap_x(pair, 0)
    return [pair, far, swap_core(pair), swap_core(far)]


def finish_kernel(*refs):
    total_ref, square_hbm, square_ref, sem = refs[2 * CHUNKS :]
    wide = HID // CHUNKS
    for c in range(CHUNKS):
        total = refs[c][...].astype(f32) + refs[CHUNKS + c][...].astype(f32)
        total_ref[:, c * wide : (c + 1) * wide] = total.astype(bf16)
        square = jnp.sum(total * total, axis=0, keepdims=True)
        square = square if c == 0 else before + square
        before = square
    square_ref[...] = jnp.broadcast_to(jnp.sum(square, axis=1, keepdims=True), (8, 128))[None] + jnp.zeros(square_ref.shape, f32)
    leave = pltpu.make_async_copy(square_ref, square_hbm, sem)
    leave.start()
    leave.wait()


def fetch(sources, targets, sem):
    copies = [pltpu.make_async_copy(a, b, sem.at[i]) for i, (a, b) in enumerate(zip(sources, targets))]
    for copy in copies:
        copy.start()
    return copies


def rates_of(block, meta_ref, rate_ref):
    count = rate_ref.shape[1]
    position = meta_ref[0] + lax.broadcasted_iota(jnp.int32, (1, count), 1)
    mine = (position < meta_ref[2]) if block == 0 else (position >= meta_ref[2])
    rates = jnp.broadcast_to(jnp.where(mine, rate_ref[...], 0.0), (128, count))
    return jnp.transpose(rates)[:, 0:1]


def grads(block, meta_ref, keys_ref, targets_ref, rate_ref, wb_ref, grad_ref, outs, ready=lambda what: None):
    place = meta_ref[3]
    rates = rates_of(block, meta_ref, rate_ref)
    ready(3)
    keys = keys_ref[...]
    d_out = None
    half, wide = ROWS // 2, HID // CHUNKS
    for c in range(CHUNKS):
        cols = slice(c * wide, (c + 1) * wide)
        if c == 0:
            ready(0)
        first = dot(keys, wb_ref[0:HD, cols], 1, 0)
        if c == 0:
            ready(1)
        third = dot(keys, wb_ref[HD : 2 * HD, cols], 1, 0)
        if c == 0:
            ready(4)
            d_out = (-rates * targets_ref[...].astype(f32)).astype(bf16)
            ready(2)
        d_act = dot(d_out, wb_ref[2 * HD :, cols], 1, 0)
        sigma = jax.nn.sigmoid(first)
        swish = first * sigma
        act = (swish * third).astype(bf16)
        d_first = (d_act * third * sigma * (1.0 + first * (1.0 - sigma))).astype(bf16)
        d_third = (d_act * swish).astype(bf16)
        grad_ref[0:HD] = dot(keys, d_first, 0, 0)
        grad_ref[HD : 2 * HD] = dot(keys, d_third, 0, 0)
        grad_ref[2 * HD :] = dot(d_out, act, 0, 0)
        outs[c][...] = grad_ref[pl.ds(pl.multiple_of((1 - place) * half, half), half)].astype(bf16)
        outs[CHUNKS + c][...] = grad_ref[pl.ds(pl.multiple_of(place * half, half), half)]


def first_kernel(meta_ref, keys_hbm, targets_hbm, rate_ref, w_hbm, wb_hbm, *rest):
    outs, (grad_ref, keys_ref, targets_ref, w_ref, wb_ref, sem) = rest[: 2 * CHUNKS], rest[2 * CHUNKS :]
    thirds = [pl.ds(i * HD, HD) for i in range(3)]
    sources = [w_hbm.at[t] for t in thirds] + [keys_hbm, targets_hbm]
    targets = [w_ref.at[t] for t in thirds] + [keys_ref, targets_ref]
    copies = [pltpu.make_async_copy(a, b, sem.at[i]) for i, (a, b) in enumerate(zip(sources, targets))]
    for i in (3, 0, 1, 4, 2):
        copies[i].start()

    def ready(what):
        copies[what].wait()
        if what < 3:
            wb_ref[thirds[what]] = w_ref[thirds[what]].astype(bf16)
        if what == 2:
            leave.start()

    leave = pltpu.make_async_copy(wb_ref, wb_hbm, sem.at[5])
    grads(0, meta_ref, keys_ref, targets_ref, rate_ref, wb_ref, grad_ref, outs, ready)
    leave.wait()


def piece_rows(starts_ref):
    rows = ROWS // 8
    return [pl.ds(pl.multiple_of(starts_ref[i], rows), rows) for i in range(8)]


def renew(starts_ref, square_ref, w_ref, pieces, new_ref, out_ref, sem, wb_ref=None, arrive=None):
    mean = jnp.sum(square_ref[...], axis=0)[0:1, 0:1] / float(HEADS * ROWS * HID)
    factor = fast_rate / jnp.sqrt(mean + epsilon)
    rows = ROWS // 8
    copies = []
    for i, at in enumerate(piece_rows(starts_ref)):
        if arrive is not None:
            arrive[i].wait()
        new = w_ref[at] - factor * pieces[i // 2][i % 2 * rows : (i % 2 + 1) * rows].astype(f32)
        new_ref[at] = new
        copies.append(pltpu.make_async_copy(new_ref.at[at], out_ref.at[at], sem.at[i]))
        copies[-1].start()
        if wb_ref is not None:
            wb_ref[at] = new.astype(bf16)
    return copies


def second_kernel(meta_ref, starts_ref, square_ref, keys_hbm, targets_hbm, rate_ref, w_hbm, *rest):
    pieces, (out_ref, wb_ref, *outs) = rest[:4], rest[4 : 6 + 2 * CHUNKS]
    grad_ref, new_ref, sem, keys_ref, targets_ref, w_ref, fetched = rest[6 + 2 * CHUNKS :]
    spans = piece_rows(starts_ref)
    arrive = fetch(
        [w_hbm.at[at] for at in spans] + [keys_hbm, targets_hbm],
        [w_ref.at[at] for at in spans] + [keys_ref, targets_ref],
        fetched,
    )
    copies = renew(starts_ref, square_ref, w_ref, pieces, new_ref, out_ref, sem, wb_ref, arrive)
    for copy in arrive[8:]:
        copy.wait()
    grads(1, meta_ref, keys_ref, targets_ref, rate_ref, wb_ref, grad_ref, outs)
    for copy in copies:
        copy.wait()


def last_kernel(starts_ref, square_ref, w_ref, *rest):
    pieces, (out_ref, new_ref, sem) = rest[:4], rest[4:]
    for copy in renew(starts_ref, square_ref, w_ref, pieces, new_ref, out_ref, sem):
        copy.wait()


def attend_kernel(meta_ref, q_ref, halo_ref, k_ref, late_v_ref, v_ref, out_ref, halo_v_ref):
    local = q_ref.shape[0]
    anchor, width = meta_ref[0], meta_ref[1]
    scale = HD ** (-0.5)
    halo_v_ref[0:EARLY] = halo_ref[WIN:]
    halo_v_ref[EARLY:] = late_v_ref[...]
    held = [(halo_ref, halo_v_ref, -WIN, WIN), (k_ref, v_ref, 0, local)]
    for start in range(0, local, TILE):
        spans = []
        for keys, values, base, count in held:
            low, high = max(base, start - WIN), min(base + count, start + TILE)
            if low < high:
                spans.append((keys, values, low - base, high - base, low))
        query = q_ref[start : start + TILE]
        scores = []
        for keys, _, low, high, position in spans:
            s = dot(query, keys[low:high], 1, 1) * scale
            row = lax.broadcasted_iota(jnp.int32, s.shape, 0) + start
            col = lax.broadcasted_iota(jnp.int32, s.shape, 1) + position
            live = (col <= row) & (col > row - width) & (col >= -anchor)
            scores.append(jnp.where(live, s, -1e30))
        peak = functools.reduce(jnp.maximum, [jnp.max(s, axis=1, keepdims=True) for s in scores])
        expo = [jnp.exp(s - peak) for s in scores]
        total = sum(jnp.sum(e, axis=1, keepdims=True) for e in expo)
        inverse = 1.0 / total
        attn = 0.0
        for e, (_, values, low, high, _) in zip(expo, spans):
            attn = attn + dot((e * inverse).astype(bf16), values[low:high], 1, 0)
        out_ref[start : start + TILE] = attn


def apply_kernel(meta_ref, q_ref, attn_ref, early_ref, late_ref, out_ref, y_ref):
    anchor, split = meta_ref[0], meta_ref[2]

    def fast(query, wb_ref):
        first = dot(query, wb_ref[0:HD], 1, 0)
        third = dot(query, wb_ref[HD : 2 * HD], 1, 0)
        act = (first * jax.nn.sigmoid(first) * third).astype(bf16)
        return dot(act, wb_ref[2 * HD :], 1, 1)

    def tile(i, carry):
        start = pl.multiple_of(i * TILE, TILE)
        rows = pl.ds(start, TILE)

        @pl.when(anchor + start < split)
        def _():
            y_ref[...] = fast(q_ref[rows], early_ref)

        @pl.when(anchor + start + TILE > split)
        def _():
            late = fast(q_ref[rows], late_ref)
            position = anchor + start + lax.broadcasted_iota(jnp.int32, late.shape, 0)
            y_ref[...] = jnp.where(position < split, y_ref[...], late)

        y = y_ref[...]
        norm = y / jnp.sqrt(jnp.mean(y * y, axis=1, keepdims=True) + epsilon)
        out_ref[rows] = (attn_ref[rows] + norm).astype(bf16)
        return carry

    lax.fori_loop(0, q_ref.shape[0] // TILE, tile, 0)


def call(kernel, specs, outs, args, megabytes, scratch=(), out_specs=None):
    return pl.pallas_call(
        kernel,
        out_shape=outs,
        in_specs=specs,
        out_specs=jax.tree.map(lambda _: VMEM_SPEC, outs) if out_specs is None else out_specs,
        scratch_shapes=list(scratch),
        compiler_params=pltpu.CompilerParams(vmem_limit_bytes=megabytes << 20),
    )(*args)


def in_hbm(value):
    return pltpu.with_memory_space_constraint(value, pltpu.HBM)


def array(shape, dtype):
    return jax.ShapeDtypeStruct(shape, dtype)


def per_device(queries, keys, values, targets, token_rate, window, split, fast_init):
    local = queries.shape[0]
    anchor = lax.axis_index(SEQ) * local
    count = lax.axis_size(SEQ)
    onward = [(i, i + 1) for i in range(count - 1)]
    tail = local - WIN
    halo_v = lax.ppermute(values[tail + EARLY :], SEQ, onward)
    with_gather = jnp.concatenate([keys[tail:], values[tail : tail + EARLY]], axis=0)
    rate = token_rate.reshape(1, local)
    starts = piece_starts()
    meta = jnp.stack([anchor, window[0], split[0], lax.axis_index("core")]).astype(jnp.int32)
    weights_zero = fast_init.reshape(ROWS, HID)
    half = ROWS // 2
    wide = [array((half, HID // CHUNKS), kind) for kind in (bf16, f32) for _ in range(CHUNKS)]
    grad = pltpu.VMEM((ROWS, HID // CHUNKS), f32)
    renewal = [pltpu.VMEM((ROWS, HID), f32), pltpu.SemaphoreType.DMA((8,))]

    fetched = [pltpu.VMEM((local, HD), bf16)] * 2

    wb_zero, *halved = call(
        first_kernel,
        [SMEM_SPEC, HBM_SPEC, HBM_SPEC, VMEM_SPEC, HBM_SPEC],
        [pltpu.HBM((ROWS, HID), bf16)] + wide,
        (meta, in_hbm(keys), in_hbm(targets), rate, in_hbm(weights_zero)),
        24,
        [grad] + fetched + [pltpu.VMEM((ROWS, HID), f32), pltpu.VMEM((ROWS, HID), bf16), pltpu.SemaphoreType.DMA((6,))],
        [HBM_SPEC] + [VMEM_SPEC] * (2 * CHUNKS),
    )

    def finished(mine, other, later):
        total, square = call(
            finish_kernel,
            [VMEM_SPEC] * (2 * CHUNKS),
            [array((ROWS // 8, HID), bf16), pltpu.HBM((SHARES, 8, 128), f32)],
            (*mine, *other),
            8,
            [pltpu.VMEM((SHARES, 8, 128), f32), pltpu.SemaphoreType.DMA],
            [VMEM_SPEC, HBM_SPEC],
        )
        if later is not None:
            total, later = lax.optimization_barrier((total, later))
        return spread(square), gathered(total), later

    kept = {}

    square, pieces, send = finished(*reduced(halved[:CHUNKS], halved[CHUNKS:]), with_gather)
    halo = lax.ppermute(send, SEQ, onward)
    weights_one, wb_one, *halved = call(
        second_kernel,
        [SMEM_SPEC] * 2 + [VMEM_SPEC, HBM_SPEC, HBM_SPEC, VMEM_SPEC, HBM_SPEC] + [VMEM_SPEC] * 4,
        [pltpu.HBM((ROWS, HID), f32), array((ROWS, HID), bf16)] + wide,
        (meta, starts, square, in_hbm(keys), in_hbm(targets), rate, in_hbm(weights_zero), *pieces),
        24,
        [grad] + renewal + fetched + [pltpu.VMEM((ROWS, HID), f32), pltpu.SemaphoreType.DMA((10,))],
        [HBM_SPEC] + [VMEM_SPEC] * (1 + 2 * CHUNKS),
    )
    kept["halo"], halved = lax.optimization_barrier((halo, halved))

    def attend(before, after):
        query, _ = lax.optimization_barrier((queries, before))
        attn = call(
            attend_kernel,
            [SMEM_SPEC] + [VMEM_SPEC] * 5,
            array((local, HD), f32),
            (meta, query, kept["halo"], keys, halo_v, values),
            20,
            [pltpu.VMEM((WIN, HD), bf16)],
        )
        kept["attn"], after = lax.optimization_barrier((attn, after))
        return after

    def apply(before, after):
        query, _ = lax.optimization_barrier((queries, before))
        outputs = call(
            apply_kernel,
            [SMEM_SPEC] + [VMEM_SPEC] * 4,
            array((local, HD), bf16),
            (meta, query, kept["attn"], wb_zero, wb_one),
            20,
            [pltpu.VMEM((TILE, HD), f32)],
        )
        kept["outputs"], after = lax.optimization_barrier((outputs, after))
        return after

    square, pieces, _ = finished(*reduced(halved[:CHUNKS], halved[CHUNKS:], attend, apply), None)
    weights_two = call(
        last_kernel,
        [SMEM_SPEC] + [VMEM_SPEC] * 6,
        array((ROWS, HID), f32),
        (starts, square, weights_one, *pieces),
        20,
        renewal,
        ANY_SPEC,
    )
    return (kept["outputs"], weights_two.reshape(1, 3, HD, HID))


def solution(mesh):
    finer = Mesh(mesh.devices.reshape(4, 4, 2, mesh.shape["head"]), ("z", "x", "core", "head"))
    tokens = P(SEQ, "head")
    weights = P("head", None, None, None)
    return jax.shard_map(
        per_device,
        mesh=finer,
        in_specs=(tokens,) * 5 + (P("head"), P(), weights),
        out_specs=(tokens, weights),
        check_vma=False,
    )
```

```python
import functools
import math

import jax
import jax.numpy as jnp
from jax import lax
from jax.experimental import pallas as pl
from jax.experimental.pallas import tpu as pltpu
from jax.sharding import Mesh
from jax.sharding import PartitionSpec as P

HEADS = 8
HD = 512
HID = 512
WIN = 512
ROWS = 3 * HD
SEQ = ("z", "x", "core")
TILE = 256
CHUNKS = 2
SHARES = 64
EARLY = 256

fast_rate = 0.01
epsilon = 1e-06
bf16 = jnp.bfloat16
f32 = jnp.float32
VMEM_SPEC = pl.BlockSpec(memory_space=pltpu.VMEM)
SMEM_SPEC = pl.BlockSpec(memory_space=pltpu.SMEM)
ANY_SPEC = pl.BlockSpec(memory_space=pl.ANY)
HBM_SPEC = pl.BlockSpec(memory_space=pltpu.HBM)


def dot(a, b, over_a, over_b):
    return lax.dot_general(a, b, (((over_a,), (over_b,)), ((), ())), preferred_element_type=f32)


def exchange(value, mesh_axes, partner):
    count = math.prod(lax.axis_size(a) for a in mesh_axes)
    return lax.ppermute(value, mesh_axes, [(i, partner(i)) for i in range(count)])


def ring_pair(step):
    def partner(i):
        place, core = divmod(i, 2)
        return (place ^ (1 if core == step else 3)) * 2 + core

    return partner


def swap_x(value, step):
    return exchange(value, ("x", "core"), ring_pair(step))


def swap_z(value, step):
    return exchange(value, ("z", "core"), ring_pair(step))


def swap_core(value):
    return exchange(value, ("core",), lambda i: i ^ 1)


def spread(squares):
    return lax.all_to_all(squares, ("x", "core", "head"), 0, 0, tiled=True)


def rows_of(value, start, count):
    return lax.dynamic_slice_in_dim(value, start, count, 0)


def halves():
    core = lax.axis_index("core")
    place = lax.axis_index("x")
    low, high = place & 1, place >> 1
    first = jnp.where(core == 0, low ^ high, high)
    second = jnp.where(core == 0, high, low ^ high)
    return core, first, second


def piece_starts():
    core, a, b = halves()
    here = [(a, b), (a, 1 - b), (1 - a, b), (1 - a, 1 - b)]
    there = [(b, a), (b, 1 - a), (1 - b, a), (1 - b, 1 - a)]
    places = [core * 4 + i * 2 + j for i, j in here] + [(1 - core) * 4 + i * 2 + j for i, j in there]
    return (jnp.stack(places) * (ROWS // 8)).astype(jnp.int32)


def reduced(sent, own, beside_first=None, beside_second=None):
    _, first, second = halves()
    half, rows = ROWS // 4, ROWS // 8
    chunks = range(len(sent))
    got = [swap_core(s) for s in sent]

    def two(c, start, count):
        return rows_of(own[c], start, count) + rows_of(got[c], start, count).astype(f32)

    got_x = [swap_x(two(c, (1 - first) * half, half).astype(bf16), 0) for c in chunks]
    away = (1 - second) * rows
    send = [(two(c, first * half + away, rows) + rows_of(got_x[c], away, rows).astype(f32)).astype(bf16) for c in chunks]
    got_x2 = [swap_x(s, 1) for s in send]
    near = second * rows
    mine = [two(c, first * half + near, rows) + rows_of(got_x[c], near, rows).astype(f32) + got_x2[c].astype(f32) for c in chunks]
    mine = [m.astype(bf16) for m in mine]
    other = [swap_z(m, 0) for m in mine]
    if beside_first is not None:
        other = beside_first(mine, other)
    mine = [(m.astype(f32) + o.astype(f32)).astype(bf16) for m, o in zip(mine, other)]
    other = [swap_z(m, 1) for m in mine]
    if beside_second is not None:
        other = beside_second(mine, other)
    return mine, other


def gathered(own, squares):
    near = swap_x(own, 1)
    pair = jnp.concatenate([own, near], axis=0)
    far = swap_x(pair, 0)
    far, squares = lax.optimization_barrier((far, squares))
    return squares, [pair, far, swap_core(pair), swap_core(far)]


def finish_kernel(*refs):
    total_ref, square_hbm, square_ref, sem = refs[2 * CHUNKS :]
    wide = HID // CHUNKS
    for c in range(CHUNKS):
        total = refs[c][...].astype(f32) + refs[CHUNKS + c][...].astype(f32)
        total_ref[:, c * wide : (c + 1) * wide] = total.astype(bf16)
        square = jnp.sum(total * total, axis=0, keepdims=True)
        square = square if c == 0 else before + square
        before = square
    square_ref[...] = jnp.broadcast_to(jnp.sum(square, axis=1, keepdims=True), (8, 128))[None] + jnp.zeros(square_ref.shape, f32)
    leave = pltpu.make_async_copy(square_ref, square_hbm, sem)
    leave.start()
    leave.wait()


def fetch(sources, targets, sem):
    copies = [pltpu.make_async_copy(a, b, sem.at[i]) for i, (a, b) in enumerate(zip(sources, targets))]
    for copy in copies:
        copy.start()
    return copies


def grads(place, keys_ref, targets_ref, rate_ref, wb_ref, grad_ref, outs):
    keys = keys_ref[...]
    d_out = (-rate_ref[...] * targets_ref[...].astype(f32)).astype(bf16)
    half, wide = ROWS // 2, HID // CHUNKS
    for c in range(CHUNKS):
        cols = slice(c * wide, (c + 1) * wide)
        first = dot(keys, wb_ref[0:HD, cols], 1, 0)
        third = dot(keys, wb_ref[HD : 2 * HD, cols], 1, 0)
        d_act = dot(d_out, wb_ref[2 * HD :, cols], 1, 0)
        sigma = jax.nn.sigmoid(first)
        swish = first * sigma
        act = (swish * third).astype(bf16)
        d_first = (d_act * third * sigma * (1.0 + first * (1.0 - sigma))).astype(bf16)
        d_third = (d_act * swish).astype(bf16)
        grad_ref[0:HD] = dot(keys, d_first, 0, 0)
        grad_ref[HD : 2 * HD] = dot(keys, d_third, 0, 0)
        grad_ref[2 * HD :] = dot(d_out, act, 0, 0)
        outs[c][...] = grad_ref[pl.ds(pl.multiple_of((1 - place) * half, half), half)].astype(bf16)
        outs[CHUNKS + c][...] = grad_ref[pl.ds(pl.multiple_of(place * half, half), half)]


def first_kernel(place_ref, keys_hbm, targets_hbm, rate_ref, w_hbm, wb_hbm, *rest):
    outs, (grad_ref, keys_ref, targets_ref, w_ref, wb_ref, sem) = rest[: 2 * CHUNKS], rest[2 * CHUNKS :]
    thirds = [pl.ds(i * HD, HD) for i in range(3)]
    copies = fetch(
        [w_hbm.at[t] for t in thirds] + [keys_hbm, targets_hbm],
        [w_ref.at[t] for t in thirds] + [keys_ref, targets_ref],
        sem,
    )
    for copy, third in zip(copies, thirds):
        copy.wait()
        wb_ref[third] = w_ref[third].astype(bf16)
    leave = pltpu.make_async_copy(wb_ref, wb_hbm, sem.at[5])
    leave.start()
    copies[3].wait()
    copies[4].wait()
    grads(place_ref[0], keys_ref, targets_ref, rate_ref, wb_ref, grad_ref, outs)
    leave.wait()


def piece_rows(starts_ref):
    rows = ROWS // 8
    return [pl.ds(pl.multiple_of(starts_ref[i], rows), rows) for i in range(8)]


def renew(starts_ref, square_ref, w_ref, pieces, new_ref, out_ref, sem, wb_ref=None, arrive=None):
    mean = jnp.sum(square_ref[...], axis=0)[0:1, 0:1] / float(HEADS * ROWS * HID)
    factor = fast_rate / jnp.sqrt(mean + epsilon)
    rows = ROWS // 8
    copies = []
    for i, at in enumerate(piece_rows(starts_ref)):
        if arrive is not None:
            arrive[i].wait()
        new = w_ref[at] - factor * pieces[i // 2][i % 2 * rows : (i % 2 + 1) * rows].astype(f32)
        new_ref[at] = new
        copies.append(pltpu.make_async_copy(new_ref.at[at], out_ref.at[at], sem.at[i]))
        copies[-1].start()
        if wb_ref is not None:
            wb_ref[at] = new.astype(bf16)
    return copies


def second_kernel(place_ref, starts_ref, square_ref, keys_hbm, targets_hbm, rate_ref, w_hbm, *rest):
    pieces, (out_ref, wb_ref, *outs) = rest[:4], rest[4 : 6 + 2 * CHUNKS]
    grad_ref, new_ref, sem, keys_ref, targets_ref, w_ref, fetched = rest[6 + 2 * CHUNKS :]
    spans = piece_rows(starts_ref)
    arrive = fetch(
        [w_hbm.at[at] for at in spans] + [keys_hbm, targets_hbm],
        [w_ref.at[at] for at in spans] + [keys_ref, targets_ref],
        fetched,
    )
    copies = renew(starts_ref, square_ref, w_ref, pieces, new_ref, out_ref, sem, wb_ref, arrive)
    for copy in arrive[8:]:
        copy.wait()
    grads(place_ref[0], keys_ref, targets_ref, rate_ref, wb_ref, grad_ref, outs)
    for copy in copies:
        copy.wait()


def last_kernel(starts_ref, square_ref, w_ref, *rest):
    pieces, (out_ref, new_ref, sem) = rest[:4], rest[4:]
    for copy in renew(starts_ref, square_ref, w_ref, pieces, new_ref, out_ref, sem):
        copy.wait()


def attend_kernel(meta_ref, q_ref, halo_ref, k_ref, late_v_ref, v_ref, out_ref, halo_v_ref):
    local = q_ref.shape[0]
    anchor, width = meta_ref[0], meta_ref[1]
    scale = HD ** (-0.5)
    halo_v_ref[0:EARLY] = halo_ref[WIN:]
    halo_v_ref[EARLY:] = late_v_ref[...]
    held = [(halo_ref, halo_v_ref, -WIN, WIN), (k_ref, v_ref, 0, local)]
    for start in range(0, local, TILE):
        spans = []
        for keys, values, base, count in held:
            low, high = max(base, start - WIN), min(base + count, start + TILE)
            if low < high:
                spans.append((keys, values, low - base, high - base, low))
        query = q_ref[start : start + TILE]
        scores = []
        for keys, _, low, high, position in spans:
            s = dot(query, keys[low:high], 1, 1) * scale
            row = lax.broadcasted_iota(jnp.int32, s.shape, 0) + start
            col = lax.broadcasted_iota(jnp.int32, s.shape, 1) + position
            live = (col <= row) & (col > row - width) & (col >= -anchor)
            scores.append(jnp.where(live, s, -1e30))
        peak = functools.reduce(jnp.maximum, [jnp.max(s, axis=1, keepdims=True) for s in scores])
        expo = [jnp.exp(s - peak) for s in scores]
        total = sum(jnp.sum(e, axis=1, keepdims=True) for e in expo)
        inverse = 1.0 / total
        attn = 0.0
        for e, (_, values, low, high, _) in zip(expo, spans):
            attn = attn + dot((e * inverse).astype(bf16), values[low:high], 1, 0)
        out_ref[start : start + TILE] = attn


def apply_kernel(meta_ref, q_ref, attn_ref, early_ref, late_ref, out_ref, y_ref):
    anchor, split = meta_ref[0], meta_ref[2]

    def fast(query, wb_ref):
        first = dot(query, wb_ref[0:HD], 1, 0)
        third = dot(query, wb_ref[HD : 2 * HD], 1, 0)
        act = (first * jax.nn.sigmoid(first) * third).astype(bf16)
        return dot(act, wb_ref[2 * HD :], 1, 1)

    def tile(i, carry):
        start = pl.multiple_of(i * TILE, TILE)
        rows = pl.ds(start, TILE)

        @pl.when(anchor + start < split)
        def _():
            y_ref[...] = fast(q_ref[rows], early_ref)

        @pl.when(anchor + start + TILE > split)
        def _():
            late = fast(q_ref[rows], late_ref)
            position = anchor + start + lax.broadcasted_iota(jnp.int32, late.shape, 0)
            y_ref[...] = jnp.where(position < split, y_ref[...], late)

        y = y_ref[...]
        norm = y / jnp.sqrt(jnp.mean(y * y, axis=1, keepdims=True) + epsilon)
        out_ref[rows] = (attn_ref[rows] + norm).astype(bf16)
        return carry

    lax.fori_loop(0, q_ref.shape[0] // TILE, tile, 0)


def call(kernel, specs, outs, args, megabytes, scratch=(), out_specs=None):
    return pl.pallas_call(
        kernel,
        out_shape=outs,
        in_specs=specs,
        out_specs=jax.tree.map(lambda _: VMEM_SPEC, outs) if out_specs is None else out_specs,
        scratch_shapes=list(scratch),
        compiler_params=pltpu.CompilerParams(vmem_limit_bytes=megabytes << 20),
    )(*args)


def in_hbm(value):
    return pltpu.with_memory_space_constraint(value, pltpu.HBM)


def array(shape, dtype):
    return jax.ShapeDtypeStruct(shape, dtype)


def per_device(queries, keys, values, targets, token_rate, window, split, fast_init):
    local = queries.shape[0]
    anchor = lax.axis_index(SEQ) * local
    count = lax.axis_size(SEQ)
    onward = [(i, i + 1) for i in range(count - 1)]
    tail = local - WIN
    halo_v = lax.ppermute(values[tail + EARLY :], SEQ, onward)
    with_gather = jnp.concatenate([keys[tail:], values[tail : tail + EARLY]], axis=0)
    positions = anchor + jnp.arange(local, dtype=jnp.int32)[:, None]
    first_block = (positions < split[0]).astype(f32)
    rate_zero = token_rate * first_block
    rate_one = token_rate * (1.0 - first_block)
    core = lax.axis_index("core").astype(jnp.int32).reshape(1)
    starts = piece_starts()
    meta = jnp.stack([anchor, window[0], split[0]]).astype(jnp.int32)
    weights_zero = fast_init.reshape(ROWS, HID)
    half = ROWS // 2
    wide = [array((half, HID // CHUNKS), kind) for kind in (bf16, f32) for _ in range(CHUNKS)]
    grad = pltpu.VMEM((ROWS, HID // CHUNKS), f32)
    renewal = [pltpu.VMEM((ROWS, HID), f32), pltpu.SemaphoreType.DMA((8,))]

    fetched = [pltpu.VMEM((local, HD), bf16)] * 2

    wb_zero, *halved = call(
        first_kernel,
        [SMEM_SPEC, HBM_SPEC, HBM_SPEC, VMEM_SPEC, HBM_SPEC],
        [pltpu.HBM((ROWS, HID), bf16)] + wide,
        (core, in_hbm(keys), in_hbm(targets), rate_zero, in_hbm(weights_zero)),
        24,
        [grad] + fetched + [pltpu.VMEM((ROWS, HID), f32), pltpu.VMEM((ROWS, HID), bf16), pltpu.SemaphoreType.DMA((6,))],
        [HBM_SPEC] + [VMEM_SPEC] * (2 * CHUNKS),
    )

    def finished(mine, other, later):
        total, square = call(
            finish_kernel,
            [VMEM_SPEC] * (2 * CHUNKS),
            [array((ROWS // 8, HID), bf16), pltpu.HBM((SHARES, 8, 128), f32)],
            (*mine, *other),
            8,
            [pltpu.VMEM((SHARES, 8, 128), f32), pltpu.SemaphoreType.DMA],
            [VMEM_SPEC, HBM_SPEC],
        )
        if later is not None:
            total, later = lax.optimization_barrier((total, later))
        return *gathered(total, spread(square)), later

    kept = {}

    square, pieces, send = finished(*reduced(halved[:CHUNKS], halved[CHUNKS:]), with_gather)
    halo = lax.ppermute(send, SEQ, onward)
    weights_one, wb_one, *halved = call(
        second_kernel,
        [SMEM_SPEC] * 2 + [VMEM_SPEC, HBM_SPEC, HBM_SPEC, VMEM_SPEC, HBM_SPEC] + [VMEM_SPEC] * 4,
        [pltpu.HBM((ROWS, HID), f32), array((ROWS, HID), bf16)] + wide,
        (core, starts, square, in_hbm(keys), in_hbm(targets), rate_one, in_hbm(weights_zero), *pieces),
        24,
        [grad] + renewal + fetched + [pltpu.VMEM((ROWS, HID), f32), pltpu.SemaphoreType.DMA((10,))],
        [HBM_SPEC] + [VMEM_SPEC] * (1 + 2 * CHUNKS),
    )
    kept["halo"], halved = lax.optimization_barrier((halo, halved))

    def attend(before, after):
        query, _ = lax.optimization_barrier((queries, before))
        attn = call(
            attend_kernel,
            [SMEM_SPEC] + [VMEM_SPEC] * 5,
            array((local, HD), f32),
            (meta, query, kept["halo"], keys, halo_v, values),
            20,
            [pltpu.VMEM((WIN, HD), bf16)],
        )
        kept["attn"], after = lax.optimization_barrier((attn, after))
        return after

    def apply(before, after):
        query, _ = lax.optimization_barrier((queries, before))
        outputs = call(
            apply_kernel,
            [SMEM_SPEC] + [VMEM_SPEC] * 4,
            array((local, HD), bf16),
            (meta, query, kept["attn"], wb_zero, wb_one),
            20,
            [pltpu.VMEM((TILE, HD), f32)],
        )
        kept["outputs"], after = lax.optimization_barrier((outputs, after))
        return after

    square, pieces, _ = finished(*reduced(halved[:CHUNKS], halved[CHUNKS:], attend, apply), None)
    weights_two = call(
        last_kernel,
        [SMEM_SPEC] + [VMEM_SPEC] * 6,
        array((ROWS, HID), f32),
        (starts, square, weights_one, *pieces),
        20,
        renewal,
        ANY_SPEC,
    )
    return (kept["outputs"], weights_two.reshape(1, 3, HD, HID))


def solution(mesh):
    finer = Mesh(mesh.devices.reshape(4, 4, 2, mesh.shape["head"]), ("z", "x", "core", "head"))
    tokens = P(SEQ, "head")
    weights = P("head", None, None, None)
    return jax.shard_map(
        per_device,
        mesh=finer,
        in_specs=(tokens,) * 5 + (P("head"), P(), weights),
        out_specs=(tokens, weights),
        check_vma=False,
    )
```

```python
import functools
import math

import jax
import jax.numpy as jnp
from jax import lax
from jax.experimental import pallas as pl
from jax.experimental.pallas import tpu as pltpu
from jax.sharding import Mesh
from jax.sharding import PartitionSpec as P

HEADS = 8
HD = 512
HID = 512
WIN = 512
ROWS = 3 * HD
SEQ = ("z", "x", "core")
TILE = 256
CHUNKS = 2
SHARES = 64
EARLY = 256

fast_rate = 0.01
epsilon = 1e-06
bf16 = jnp.bfloat16
f32 = jnp.float32
VMEM_SPEC = pl.BlockSpec(memory_space=pltpu.VMEM)
SMEM_SPEC = pl.BlockSpec(memory_space=pltpu.SMEM)
ANY_SPEC = pl.BlockSpec(memory_space=pl.ANY)
HBM_SPEC = pl.BlockSpec(memory_space=pltpu.HBM)


def dot(a, b, over_a, over_b):
    return lax.dot_general(a, b, (((over_a,), (over_b,)), ((), ())), preferred_element_type=f32)


def exchange(value, mesh_axes, partner):
    count = math.prod(lax.axis_size(a) for a in mesh_axes)
    return lax.ppermute(value, mesh_axes, [(i, partner(i)) for i in range(count)])


def ring_pair(step):
    def partner(i):
        place, core = divmod(i, 2)
        return (place ^ (1 if core == step else 3)) * 2 + core

    return partner


def swap_x(value, step):
    return exchange(value, ("x", "core"), ring_pair(step))


def swap_z(value, step):
    return exchange(value, ("z", "core"), ring_pair(step))


def swap_core(value):
    return exchange(value, ("core",), lambda i: i ^ 1)


def spread(squares):
    return lax.all_to_all(squares, ("x", "core", "head"), 0, 0, tiled=True)


def rows_of(value, start, count):
    return lax.dynamic_slice_in_dim(value, start, count, 0)


def halves():
    core = lax.axis_index("core")
    place = lax.axis_index("x")
    low, high = place & 1, place >> 1
    first = jnp.where(core == 0, low ^ high, high)
    second = jnp.where(core == 0, high, low ^ high)
    return core, first, second


def piece_starts():
    core, a, b = halves()
    here = [(a, b), (a, 1 - b), (1 - a, b), (1 - a, 1 - b)]
    there = [(b, a), (b, 1 - a), (1 - b, a), (1 - b, 1 - a)]
    places = [core * 4 + i * 2 + j for i, j in here] + [(1 - core) * 4 + i * 2 + j for i, j in there]
    return (jnp.stack(places) * (ROWS // 8)).astype(jnp.int32)


def reduced(sent, own, before_z=None, beside_first=None, beside_second=None):
    _, first, second = halves()
    half, rows = ROWS // 4, ROWS // 8
    chunks = range(len(sent))
    got = [swap_core(s) for s in sent]

    def two(c, start, count):
        return rows_of(own[c], start, count) + rows_of(got[c], start, count).astype(f32)

    got_x = [swap_x(two(c, (1 - first) * half, half).astype(bf16), 0) for c in chunks]
    away = (1 - second) * rows
    send = [(two(c, first * half + away, rows) + rows_of(got_x[c], away, rows).astype(f32)).astype(bf16) for c in chunks]
    got_x2 = [swap_x(s, 1) for s in send]
    near = second * rows
    mine = [two(c, first * half + near, rows) + rows_of(got_x[c], near, rows).astype(f32) + got_x2[c].astype(f32) for c in chunks]
    mine = [m.astype(bf16) for m in mine]
    if before_z is not None:
        mine = before_z(mine)
    other = [swap_z(m, 0) for m in mine]
    if beside_first is not None:
        other = beside_first(mine, other)
    mine = [(m.astype(f32) + o.astype(f32)).astype(bf16) for m, o in zip(mine, other)]
    other = [swap_z(m, 1) for m in mine]
    if beside_second is not None:
        other = beside_second(mine, other)
    return mine, other


def gathered(own, squares):
    near = swap_x(own, 1)
    pair = jnp.concatenate([own, near], axis=0)
    far = swap_x(pair, 0)
    far, squares = lax.optimization_barrier((far, squares))
    return squares, [pair, far, swap_core(pair), swap_core(far)]


def finish_kernel(*refs):
    total_ref, square_hbm, square_ref, sem = refs[2 * CHUNKS :]
    wide = HID // CHUNKS
    for c in range(CHUNKS):
        total = refs[c][...].astype(f32) + refs[CHUNKS + c][...].astype(f32)
        total_ref[:, c * wide : (c + 1) * wide] = total.astype(bf16)
        square = jnp.sum(total * total, axis=0, keepdims=True)
        square = square if c == 0 else before + square
        before = square
    square_ref[...] = jnp.broadcast_to(jnp.sum(square, axis=1, keepdims=True), (8, 128))[None] + jnp.zeros(square_ref.shape, f32)
    leave = pltpu.make_async_copy(square_ref, square_hbm, sem)
    leave.start()
    leave.wait()


def fetch(sources, targets, sem):
    copies = [pltpu.make_async_copy(a, b, sem.at[i]) for i, (a, b) in enumerate(zip(sources, targets))]
    for copy in copies:
        copy.start()
    return copies


def grads(place, keys_ref, targets_ref, rate_ref, wb_ref, grad_ref, outs):
    keys = keys_ref[...]
    d_out = (-rate_ref[...] * targets_ref[...].astype(f32)).astype(bf16)
    half, wide = ROWS // 2, HID // CHUNKS
    for c in range(CHUNKS):
        cols = slice(c * wide, (c + 1) * wide)
        first = dot(keys, wb_ref[0:HD, cols], 1, 0)
        third = dot(keys, wb_ref[HD : 2 * HD, cols], 1, 0)
        d_act = dot(d_out, wb_ref[2 * HD :, cols], 1, 0)
        sigma = jax.nn.sigmoid(first)
        swish = first * sigma
        act = (swish * third).astype(bf16)
        d_first = (d_act * third * sigma * (1.0 + first * (1.0 - sigma))).astype(bf16)
        d_third = (d_act * swish).astype(bf16)
        grad_ref[0:HD] = dot(keys, d_first, 0, 0)
        grad_ref[HD : 2 * HD] = dot(keys, d_third, 0, 0)
        grad_ref[2 * HD :] = dot(d_out, act, 0, 0)
        outs[c][...] = grad_ref[pl.ds(pl.multiple_of((1 - place) * half, half), half)].astype(bf16)
        outs[CHUNKS + c][...] = grad_ref[pl.ds(pl.multiple_of(place * half, half), half)]


def first_kernel(place_ref, keys_hbm, targets_hbm, rate_ref, w_hbm, wb_hbm, *rest):
    outs, (grad_ref, keys_ref, targets_ref, w_ref, wb_ref, sem) = rest[: 2 * CHUNKS], rest[2 * CHUNKS :]
    thirds = [pl.ds(i * HD, HD) for i in range(3)]
    copies = fetch(
        [w_hbm.at[t] for t in thirds] + [keys_hbm, targets_hbm],
        [w_ref.at[t] for t in thirds] + [keys_ref, targets_ref],
        sem,
    )
    for copy, third in zip(copies, thirds):
        copy.wait()
        wb_ref[third] = w_ref[third].astype(bf16)
    leave = pltpu.make_async_copy(wb_ref, wb_hbm, sem.at[5])
    leave.start()
    copies[3].wait()
    copies[4].wait()
    grads(place_ref[0], keys_ref, targets_ref, rate_ref, wb_ref, grad_ref, outs)
    leave.wait()


def piece_rows(starts_ref):
    rows = ROWS // 8
    return [pl.ds(pl.multiple_of(starts_ref[i], rows), rows) for i in range(8)]


def renew(starts_ref, square_ref, w_ref, pieces, new_ref, out_ref, sem, wb_ref=None, arrive=None):
    mean = jnp.sum(square_ref[...], axis=0)[0:1, 0:1] / float(HEADS * ROWS * HID)
    factor = fast_rate / jnp.sqrt(mean + epsilon)
    rows = ROWS // 8
    copies = []
    for i, at in enumerate(piece_rows(starts_ref)):
        if arrive is not None:
            arrive[i].wait()
        new = w_ref[at] - factor * pieces[i // 2][i % 2 * rows : (i % 2 + 1) * rows].astype(f32)
        new_ref[at] = new
        copies.append(pltpu.make_async_copy(new_ref.at[at], out_ref.at[at], sem.at[i]))
        copies[-1].start()
        if wb_ref is not None:
            wb_ref[at] = new.astype(bf16)
    return copies


def second_kernel(place_ref, starts_ref, square_ref, keys_hbm, targets_hbm, rate_ref, w_hbm, *rest):
    pieces, (out_ref, wb_ref, *outs) = rest[:4], rest[4 : 6 + 2 * CHUNKS]
    grad_ref, new_ref, sem, keys_ref, targets_ref, w_ref, fetched = rest[6 + 2 * CHUNKS :]
    spans = piece_rows(starts_ref)
    arrive = fetch(
        [w_hbm.at[at] for at in spans] + [keys_hbm, targets_hbm],
        [w_ref.at[at] for at in spans] + [keys_ref, targets_ref],
        fetched,
    )
    copies = renew(starts_ref, square_ref, w_ref, pieces, new_ref, out_ref, sem, wb_ref, arrive)
    for copy in arrive[8:]:
        copy.wait()
    grads(place_ref[0], keys_ref, targets_ref, rate_ref, wb_ref, grad_ref, outs)
    for copy in copies:
        copy.wait()


def last_kernel(starts_ref, square_ref, w_hbm, *rest):
    pieces, (out_ref, new_ref, sem, w_ref, fetched) = rest[:4], rest[4:]
    spans = piece_rows(starts_ref)
    arrive = fetch([w_hbm.at[at] for at in spans], [w_ref.at[at] for at in spans], fetched)
    for copy in renew(starts_ref, square_ref, w_ref, pieces, new_ref, out_ref, sem, None, arrive):
        copy.wait()


def attend_kernel(meta_ref, q_ref, first_k_ref, halo_ref, k_ref, late_v_ref, v_ref, out_ref, halo_k_ref, halo_v_ref):
    local = q_ref.shape[0]
    anchor, width = meta_ref[0], meta_ref[1]
    scale = HD ** (-0.5)
    halo_k_ref[0:EARLY] = first_k_ref[...]
    halo_k_ref[EARLY:] = halo_ref[: WIN - EARLY]
    halo_v_ref[0:EARLY] = halo_ref[WIN - EARLY :]
    halo_v_ref[EARLY:] = late_v_ref[...]
    held = [(halo_k_ref, halo_v_ref, -WIN, WIN), (k_ref, v_ref, 0, local)]
    for start in range(0, local, TILE):
        spans = []
        for keys, values, base, count in held:
            low, high = max(base, start - WIN), min(base + count, start + TILE)
            if low < high:
                spans.append((keys, values, low - base, high - base, low))
        query = q_ref[start : start + TILE]
        scores = []
        for keys, _, low, high, position in spans:
            s = dot(query, keys[low:high], 1, 1) * scale
            row = lax.broadcasted_iota(jnp.int32, s.shape, 0) + start
            col = lax.broadcasted_iota(jnp.int32, s.shape, 1) + position
            live = (col <= row) & (col > row - width) & (col >= -anchor)
            scores.append(jnp.where(live, s, -1e30))
        peak = functools.reduce(jnp.maximum, [jnp.max(s, axis=1, keepdims=True) for s in scores])
        expo = [jnp.exp(s - peak) for s in scores]
        total = sum(jnp.sum(e, axis=1, keepdims=True) for e in expo)
        inverse = 1.0 / total
        attn = 0.0
        for e, (_, values, low, high, _) in zip(expo, spans):
            attn = attn + dot((e * inverse).astype(bf16), values[low:high], 1, 0)
        out_ref[start : start + TILE] = attn


def apply_kernel(meta_ref, q_ref, attn_ref, early_ref, late_ref, out_ref, y_ref):
    anchor, split = meta_ref[0], meta_ref[2]

    def fast(query, wb_ref):
        first = dot(query, wb_ref[0:HD], 1, 0)
        third = dot(query, wb_ref[HD : 2 * HD], 1, 0)
        act = (first * jax.nn.sigmoid(first) * third).astype(bf16)
        return dot(act, wb_ref[2 * HD :], 1, 1)

    def tile(i, carry):
        start = pl.multiple_of(i * TILE, TILE)
        rows = pl.ds(start, TILE)

        @pl.when(anchor + start < split)
        def _():
            y_ref[...] = fast(q_ref[rows], early_ref)

        @pl.when(anchor + start + TILE > split)
        def _():
            late = fast(q_ref[rows], late_ref)
            position = anchor + start + lax.broadcasted_iota(jnp.int32, late.shape, 0)
            y_ref[...] = jnp.where(position < split, y_ref[...], late)

        y = y_ref[...]
        norm = y / jnp.sqrt(jnp.mean(y * y, axis=1, keepdims=True) + epsilon)
        out_ref[rows] = (attn_ref[rows] + norm).astype(bf16)
        return carry

    lax.fori_loop(0, q_ref.shape[0] // TILE, tile, 0)


def call(kernel, specs, outs, args, megabytes, scratch=(), out_specs=None):
    return pl.pallas_call(
        kernel,
        out_shape=outs,
        in_specs=specs,
        out_specs=jax.tree.map(lambda _: VMEM_SPEC, outs) if out_specs is None else out_specs,
        scratch_shapes=list(scratch),
        compiler_params=pltpu.CompilerParams(vmem_limit_bytes=megabytes << 20),
    )(*args)


def in_hbm(value):
    return pltpu.with_memory_space_constraint(value, pltpu.HBM)


def array(shape, dtype):
    return jax.ShapeDtypeStruct(shape, dtype)


def per_device(queries, keys, values, targets, token_rate, window, split, fast_init):
    local = queries.shape[0]
    anchor = lax.axis_index(SEQ) * local
    count = lax.axis_size(SEQ)
    onward = [(i, i + 1) for i in range(count - 1)]
    tail = local - WIN
    halo_v = lax.ppermute(values[tail + EARLY :], SEQ, onward)
    halo_first = lax.ppermute(keys[tail : tail + EARLY], SEQ, onward)
    with_gather = jnp.concatenate([keys[tail + EARLY :], values[tail : tail + EARLY]], axis=0)
    positions = anchor + jnp.arange(local, dtype=jnp.int32)[:, None]
    first_block = (positions < split[0]).astype(f32)
    rate_zero = token_rate * first_block
    rate_one = token_rate * (1.0 - first_block)
    core = lax.axis_index("core").astype(jnp.int32).reshape(1)
    starts = piece_starts()
    meta = jnp.stack([anchor, window[0], split[0]]).astype(jnp.int32)
    weights_zero = fast_init.reshape(ROWS, HID)
    half = ROWS // 2
    wide = [array((half, HID // CHUNKS), kind) for kind in (bf16, f32) for _ in range(CHUNKS)]
    grad = pltpu.VMEM((ROWS, HID // CHUNKS), f32)
    renewal = [pltpu.VMEM((ROWS, HID), f32), pltpu.SemaphoreType.DMA((8,))]

    fetched = [pltpu.VMEM((local, HD), bf16)] * 2

    wb_zero, *halved = call(
        first_kernel,
        [SMEM_SPEC, HBM_SPEC, HBM_SPEC, VMEM_SPEC, HBM_SPEC],
        [pltpu.HBM((ROWS, HID), bf16)] + wide,
        (core, in_hbm(keys), in_hbm(targets), rate_zero, in_hbm(weights_zero)),
        24,
        [grad] + fetched + [pltpu.VMEM((ROWS, HID), f32), pltpu.VMEM((ROWS, HID), bf16), pltpu.SemaphoreType.DMA((6,))],
        [HBM_SPEC] + [VMEM_SPEC] * (2 * CHUNKS),
    )

    def finished(mine, other, later):
        total, square = call(
            finish_kernel,
            [VMEM_SPEC] * (2 * CHUNKS),
            [array((ROWS // 8, HID), bf16), pltpu.HBM((SHARES, 8, 128), f32)],
            (*mine, *other),
            8,
            [pltpu.VMEM((SHARES, 8, 128), f32), pltpu.SemaphoreType.DMA],
            [VMEM_SPEC, HBM_SPEC],
        )
        if later is not None:
            total, later = lax.optimization_barrier((total, later))
        return *gathered(total, spread(square)), later

    kept = {}

    def have_first(mine):
        kept["first"], mine = lax.optimization_barrier((halo_first, mine))
        return mine

    square, pieces, send = finished(*reduced(halved[:CHUNKS], halved[CHUNKS:], have_first), with_gather)
    halo = lax.ppermute(send, SEQ, onward)
    weights_one, wb_one, *halved = call(
        second_kernel,
        [SMEM_SPEC] * 2 + [VMEM_SPEC, HBM_SPEC, HBM_SPEC, VMEM_SPEC, HBM_SPEC] + [VMEM_SPEC] * 4,
        [pltpu.HBM((ROWS, HID), f32), array((ROWS, HID), bf16)] + wide,
        (core, starts, square, in_hbm(keys), in_hbm(targets), rate_one, in_hbm(weights_zero), *pieces),
        24,
        [grad] + renewal + fetched + [pltpu.VMEM((ROWS, HID), f32), pltpu.SemaphoreType.DMA((10,))],
        [HBM_SPEC] + [VMEM_SPEC] * (1 + 2 * CHUNKS),
    )
    kept["halo"], halved = lax.optimization_barrier((halo, halved))

    def attend(before, after):
        query, _ = lax.optimization_barrier((queries, before))
        attn = call(
            attend_kernel,
            [SMEM_SPEC] + [VMEM_SPEC] * 6,
            array((local, HD), f32),
            (meta, query, kept["first"], kept["halo"], keys, halo_v, values),
            20,
            [pltpu.VMEM((WIN, HD), bf16)] * 2,
        )
        kept["attn"], after = lax.optimization_barrier((attn, after))
        return after

    def apply(before, after):
        query, _ = lax.optimization_barrier((queries, before))
        outputs = call(
            apply_kernel,
            [SMEM_SPEC] + [VMEM_SPEC] * 4,
            array((local, HD), bf16),
            (meta, query, kept["attn"], wb_zero, wb_one),
            20,
            [pltpu.VMEM((TILE, HD), f32)],
        )
        kept["outputs"], after = lax.optimization_barrier((outputs, after))
        return after

    square, pieces, _ = finished(*reduced(halved[:CHUNKS], halved[CHUNKS:], None, attend, apply), None)
    weights_two = call(
        last_kernel,
        [SMEM_SPEC, VMEM_SPEC, HBM_SPEC] + [VMEM_SPEC] * 4,
        array((ROWS, HID), f32),
        (starts, square, in_hbm(weights_one), *pieces),
        20,
        renewal + [pltpu.VMEM((ROWS, HID), f32), pltpu.SemaphoreType.DMA((8,))],
        ANY_SPEC,
    )
    return (kept["outputs"], weights_two.reshape(1, 3, HD, HID))


def solution(mesh):
    finer = Mesh(mesh.devices.reshape(4, 4, 2, mesh.shape["head"]), ("z", "x", "core", "head"))
    tokens = P(SEQ, "head")
    weights = P("head", None, None, None)
    return jax.shard_map(
        per_device,
        mesh=finer,
        in_specs=(tokens,) * 5 + (P("head"), P(), weights),
        out_specs=(tokens, weights),
        check_vma=False,
    )
```

```python
import functools
import math

import jax
import jax.numpy as jnp
from jax import lax
from jax.experimental import pallas as pl
from jax.experimental.pallas import tpu as pltpu
from jax.sharding import Mesh
from jax.sharding import PartitionSpec as P

HEADS = 8
HD = 512
HID = 512
WIN = 512
ROWS = 3 * HD
SEQ = ("z", "x", "core")
TILE = 256
CHUNKS = 2
SHARES = 64
EARLY = 128

fast_rate = 0.01
epsilon = 1e-06
bf16 = jnp.bfloat16
f32 = jnp.float32
VMEM_SPEC = pl.BlockSpec(memory_space=pltpu.VMEM)
SMEM_SPEC = pl.BlockSpec(memory_space=pltpu.SMEM)
ANY_SPEC = pl.BlockSpec(memory_space=pl.ANY)
HBM_SPEC = pl.BlockSpec(memory_space=pltpu.HBM)


def dot(a, b, over_a, over_b):
    return lax.dot_general(a, b, (((over_a,), (over_b,)), ((), ())), preferred_element_type=f32)


def exchange(value, mesh_axes, partner):
    count = math.prod(lax.axis_size(a) for a in mesh_axes)
    return lax.ppermute(value, mesh_axes, [(i, partner(i)) for i in range(count)])


def ring_pair(step):
    def partner(i):
        place, core = divmod(i, 2)
        return (place ^ (1 if core == step else 3)) * 2 + core

    return partner


def swap_x(value, step):
    return exchange(value, ("x", "core"), ring_pair(step))


def swap_z(value, step):
    return exchange(value, ("z", "core"), ring_pair(step))


def swap_core(value):
    return exchange(value, ("core",), lambda i: i ^ 1)


def spread(squares):
    return lax.all_to_all(squares, ("x", "core", "head"), 0, 0, tiled=True)


def rows_of(value, start, count):
    return lax.dynamic_slice_in_dim(value, start, count, 0)


def halves():
    core = lax.axis_index("core")
    place = lax.axis_index("x")
    low, high = place & 1, place >> 1
    first = jnp.where(core == 0, low ^ high, high)
    second = jnp.where(core == 0, high, low ^ high)
    return core, first, second


def piece_starts():
    core, a, b = halves()
    here = [(a, b), (a, 1 - b), (1 - a, b), (1 - a, 1 - b)]
    there = [(b, a), (b, 1 - a), (1 - b, a), (1 - b, 1 - a)]
    places = [core * 4 + i * 2 + j for i, j in here] + [(1 - core) * 4 + i * 2 + j for i, j in there]
    return (jnp.stack(places) * (ROWS // 8)).astype(jnp.int32)


def reduced(sent, own, beside_first=None, beside_second=None):
    _, first, second = halves()
    half, rows = ROWS // 4, ROWS // 8
    chunks = range(len(sent))
    got = [swap_core(s) for s in sent]

    def two(c, start, count):
        return rows_of(own[c], start, count) + rows_of(got[c], start, count).astype(f32)

    got_x = [swap_x(two(c, (1 - first) * half, half).astype(bf16), 0) for c in chunks]
    away = (1 - second) * rows
    send = [(two(c, first * half + away, rows) + rows_of(got_x[c], away, rows).astype(f32)).astype(bf16) for c in chunks]
    got_x2 = [swap_x(s, 1) for s in send]
    near = second * rows
    mine = [two(c, first * half + near, rows) + rows_of(got_x[c], near, rows).astype(f32) + got_x2[c].astype(f32) for c in chunks]
    mine = [m.astype(bf16) for m in mine]
    other = [swap_z(m, 0) for m in mine]
    if beside_first is not None:
        other = beside_first(mine, other)
    mine = [(m.astype(f32) + o.astype(f32)).astype(bf16) for m, o in zip(mine, other)]
    other = [swap_z(m, 1) for m in mine]
    if beside_second is not None:
        other = beside_second(mine, other)
    return mine, other


def gathered(own, squares):
    near = swap_x(own, 1)
    pair = jnp.concatenate([own, near], axis=0)
    far = swap_x(pair, 0)
    far, squares = lax.optimization_barrier((far, squares))
    return squares, [pair, far, swap_core(pair), swap_core(far)]


def finish_kernel(*refs):
    total_ref, square_hbm, square_ref, sem = refs[2 * CHUNKS :]
    wide = HID // CHUNKS
    for c in range(CHUNKS):
        total = refs[c][...].astype(f32) + refs[CHUNKS + c][...].astype(f32)
        total_ref[:, c * wide : (c + 1) * wide] = total.astype(bf16)
        square = jnp.sum(total * total, axis=0, keepdims=True)
        square = square if c == 0 else before + square
        before = square
    square_ref[...] = jnp.broadcast_to(jnp.sum(square, axis=1, keepdims=True), (8, 128))[None] + jnp.zeros(square_ref.shape, f32)
    leave = pltpu.make_async_copy(square_ref, square_hbm, sem)
    leave.start()
    leave.wait()


def fetch(sources, targets, sem):
    copies = [pltpu.make_async_copy(a, b, sem.at[i]) for i, (a, b) in enumerate(zip(sources, targets))]
    for copy in copies:
        copy.start()
    return copies


def grads(place, keys_ref, targets_ref, rate_ref, wb_ref, grad_ref, outs):
    keys = keys_ref[...]
    d_out = (-rate_ref[...] * targets_ref[...].astype(f32)).astype(bf16)
    half, wide = ROWS // 2, HID // CHUNKS
    for c in range(CHUNKS):
        cols = slice(c * wide, (c + 1) * wide)
        first = dot(keys, wb_ref[0:HD, cols], 1, 0)
        third = dot(keys, wb_ref[HD : 2 * HD, cols], 1, 0)
        d_act = dot(d_out, wb_ref[2 * HD :, cols], 1, 0)
        sigma = jax.nn.sigmoid(first)
        swish = first * sigma
        act = (swish * third).astype(bf16)
        d_first = (d_act * third * sigma * (1.0 + first * (1.0 - sigma))).astype(bf16)
        d_third = (d_act * swish).astype(bf16)
        grad_ref[0:HD] = dot(keys, d_first, 0, 0)
        grad_ref[HD : 2 * HD] = dot(keys, d_third, 0, 0)
        grad_ref[2 * HD :] = dot(d_out, act, 0, 0)
        outs[c][...] = grad_ref[pl.ds(pl.multiple_of((1 - place) * half, half), half)].astype(bf16)
        outs[CHUNKS + c][...] = grad_ref[pl.ds(pl.multiple_of(place * half, half), half)]


def first_kernel(place_ref, keys_hbm, targets_hbm, values_hbm, rate_ref, w_hbm, wb_hbm, mid_hbm, late_hbm, *rest):
    outs, (grad_ref, keys_ref, targets_ref, w_ref, wb_ref, sem) = rest[: 2 * CHUNKS], rest[2 * CHUNKS :]
    thirds = [pl.ds(i * HD, HD) for i in range(3)]
    copies = fetch(
        [w_hbm.at[t] for t in thirds] + [keys_hbm, targets_hbm],
        [w_ref.at[t] for t in thirds] + [keys_ref, targets_ref],
        sem,
    )
    tail = keys_hbm.shape[0] - WIN
    tails = [
        (keys_hbm.at[pl.ds(tail, WIN)], mid_hbm.at[pl.ds(0, WIN)]),
        (values_hbm.at[pl.ds(tail, EARLY)], mid_hbm.at[pl.ds(WIN, EARLY)]),
        (values_hbm.at[pl.ds(tail + EARLY, WIN - EARLY)], late_hbm),
    ]
    moves = [pltpu.make_async_copy(a, b, sem.at[6 + i]) for i, (a, b) in enumerate(tails)]
    for move in moves:
        move.start()
    for copy, third in zip(copies, thirds):
        copy.wait()
        wb_ref[third] = w_ref[third].astype(bf16)
    leave = pltpu.make_async_copy(wb_ref, wb_hbm, sem.at[5])
    leave.start()
    copies[3].wait()
    copies[4].wait()
    grads(place_ref[0], keys_ref, targets_ref, rate_ref, wb_ref, grad_ref, outs)
    leave.wait()
    for move in moves:
        move.wait()


def piece_rows(starts_ref):
    rows = ROWS // 8
    return [pl.ds(pl.multiple_of(starts_ref[i], rows), rows) for i in range(8)]


def renew(starts_ref, square_ref, w_ref, pieces, new_ref, out_ref, sem, wb_ref=None, arrive=None):
    mean = jnp.sum(square_ref[...], axis=0)[0:1, 0:1] / float(HEADS * ROWS * HID)
    factor = fast_rate / jnp.sqrt(mean + epsilon)
    rows = ROWS // 8
    copies = []
    for i, at in enumerate(piece_rows(starts_ref)):
        if arrive is not None:
            arrive[i].wait()
        new = w_ref[at] - factor * pieces[i // 2][i % 2 * rows : (i % 2 + 1) * rows].astype(f32)
        new_ref[at] = new
        copies.append(pltpu.make_async_copy(new_ref.at[at], out_ref.at[at], sem.at[i]))
        copies[-1].start()
        if wb_ref is not None:
            wb_ref[at] = new.astype(bf16)
    return copies


def second_kernel(place_ref, starts_ref, square_ref, keys_hbm, targets_hbm, rate_ref, w_hbm, *rest):
    pieces, (out_ref, wb_ref, *outs) = rest[:4], rest[4 : 6 + 2 * CHUNKS]
    grad_ref, new_ref, sem, keys_ref, targets_ref, w_ref, fetched = rest[6 + 2 * CHUNKS :]
    spans = piece_rows(starts_ref)
    arrive = fetch(
        [w_hbm.at[at] for at in spans] + [keys_hbm, targets_hbm],
        [w_ref.at[at] for at in spans] + [keys_ref, targets_ref],
        fetched,
    )
    copies = renew(starts_ref, square_ref, w_ref, pieces, new_ref, out_ref, sem, wb_ref, arrive)
    for copy in arrive[8:]:
        copy.wait()
    grads(place_ref[0], keys_ref, targets_ref, rate_ref, wb_ref, grad_ref, outs)
    for copy in copies:
        copy.wait()


def last_kernel(starts_ref, square_ref, w_hbm, *rest):
    pieces, (out_ref, new_ref, sem, w_ref, fetched) = rest[:4], rest[4:]
    spans = piece_rows(starts_ref)
    arrive = fetch([w_hbm.at[at] for at in spans], [w_ref.at[at] for at in spans], fetched)
    for copy in renew(starts_ref, square_ref, w_ref, pieces, new_ref, out_ref, sem, None, arrive):
        copy.wait()


def attend_kernel(meta_ref, q_ref, halo_ref, k_ref, late_v_ref, v_ref, out_ref, halo_v_ref):
    local = q_ref.shape[0]
    anchor, width = meta_ref[0], meta_ref[1]
    scale = HD ** (-0.5)
    halo_v_ref[0:EARLY] = halo_ref[WIN:]
    halo_v_ref[EARLY:] = late_v_ref[...]
    held = [(halo_ref, halo_v_ref, -WIN, WIN), (k_ref, v_ref, 0, local)]
    for start in range(0, local, TILE):
        spans = []
        for keys, values, base, count in held:
            low, high = max(base, start - WIN), min(base + count, start + TILE)
            if low < high:
                spans.append((keys, values, low - base, high - base, low))
        query = q_ref[start : start + TILE]
        scores = []
        for keys, _, low, high, position in spans:
            s = dot(query, keys[low:high], 1, 1) * scale
            row = lax.broadcasted_iota(jnp.int32, s.shape, 0) + start
            col = lax.broadcasted_iota(jnp.int32, s.shape, 1) + position
            live = (col <= row) & (col > row - width) & (col >= -anchor)
            scores.append(jnp.where(live, s, -1e30))
        peak = functools.reduce(jnp.maximum, [jnp.max(s, axis=1, keepdims=True) for s in scores])
        expo = [jnp.exp(s - peak) for s in scores]
        total = sum(jnp.sum(e, axis=1, keepdims=True) for e in expo)
        inverse = 1.0 / total
        attn = 0.0
        for e, (_, values, low, high, _) in zip(expo, spans):
            attn = attn + dot((e * inverse).astype(bf16), values[low:high], 1, 0)
        out_ref[start : start + TILE] = attn


def apply_kernel(meta_ref, q_ref, attn_ref, early_ref, late_ref, out_ref, y_ref):
    anchor, split = meta_ref[0], meta_ref[2]

    def fast(query, wb_ref):
        first = dot(query, wb_ref[0:HD], 1, 0)
        third = dot(query, wb_ref[HD : 2 * HD], 1, 0)
        act = (first * jax.nn.sigmoid(first) * third).astype(bf16)
        return dot(act, wb_ref[2 * HD :], 1, 1)

    def tile(i, carry):
        start = pl.multiple_of(i * TILE, TILE)
        rows = pl.ds(start, TILE)

        @pl.when(anchor + start < split)
        def _():
            y_ref[...] = fast(q_ref[rows], early_ref)

        @pl.when(anchor + start + TILE > split)
        def _():
            late = fast(q_ref[rows], late_ref)
            position = anchor + start + lax.broadcasted_iota(jnp.int32, late.shape, 0)
            y_ref[...] = jnp.where(position < split, y_ref[...], late)

        y = y_ref[...]
        norm = y / jnp.sqrt(jnp.mean(y * y, axis=1, keepdims=True) + epsilon)
        out_ref[rows] = (attn_ref[rows] + norm).astype(bf16)
        return carry

    lax.fori_loop(0, q_ref.shape[0] // TILE, tile, 0)


def call(kernel, specs, outs, args, megabytes, scratch=(), out_specs=None):
    return pl.pallas_call(
        kernel,
        out_shape=outs,
        in_specs=specs,
        out_specs=jax.tree.map(lambda _: VMEM_SPEC, outs) if out_specs is None else out_specs,
        scratch_shapes=list(scratch),
        compiler_params=pltpu.CompilerParams(vmem_limit_bytes=megabytes << 20),
    )(*args)


def in_hbm(value):
    return pltpu.with_memory_space_constraint(value, pltpu.HBM)


def array(shape, dtype):
    return jax.ShapeDtypeStruct(shape, dtype)


def per_device(queries, keys, values, targets, token_rate, window, split, fast_init):
    local = queries.shape[0]
    anchor = lax.axis_index(SEQ) * local
    count = lax.axis_size(SEQ)
    onward = [(i, i + 1) for i in range(count - 1)]
    positions = anchor + jnp.arange(local, dtype=jnp.int32)[:, None]
    first_block = (positions < split[0]).astype(f32)
    rate_zero = token_rate * first_block
    rate_one = token_rate * (1.0 - first_block)
    core = lax.axis_index("core").astype(jnp.int32).reshape(1)
    starts = piece_starts()
    meta = jnp.stack([anchor, window[0], split[0]]).astype(jnp.int32)
    weights_zero = fast_init.reshape(ROWS, HID)
    half = ROWS // 2
    wide = [array((half, HID // CHUNKS), kind) for kind in (bf16, f32) for _ in range(CHUNKS)]
    grad = pltpu.VMEM((ROWS, HID // CHUNKS), f32)
    renewal = [pltpu.VMEM((ROWS, HID), f32), pltpu.SemaphoreType.DMA((8,))]

    fetched = [pltpu.VMEM((local, HD), bf16)] * 2

    wb_zero, with_gather, late, *halved = call(
        first_kernel,
        [SMEM_SPEC, HBM_SPEC, HBM_SPEC, HBM_SPEC, VMEM_SPEC, HBM_SPEC],
        [pltpu.HBM((ROWS, HID), bf16), pltpu.HBM((WIN + EARLY, HD), bf16), pltpu.HBM((WIN - EARLY, HD), bf16)] + wide,
        (core, in_hbm(keys), in_hbm(targets), in_hbm(values), rate_zero, in_hbm(weights_zero)),
        24,
        [grad] + fetched + [pltpu.VMEM((ROWS, HID), f32), pltpu.VMEM((ROWS, HID), bf16), pltpu.SemaphoreType.DMA((9,))],
        [HBM_SPEC] * 3 + [VMEM_SPEC] * (2 * CHUNKS),
    )
    halo_v = lax.ppermute(late, SEQ, onward)

    def finished(mine, other, later):
        total, square = call(
            finish_kernel,
            [VMEM_SPEC] * (2 * CHUNKS),
            [array((ROWS // 8, HID), bf16), pltpu.HBM((SHARES, 8, 128), f32)],
            (*mine, *other),
            8,
            [pltpu.VMEM((SHARES, 8, 128), f32), pltpu.SemaphoreType.DMA],
            [VMEM_SPEC, HBM_SPEC],
        )
        if later is not None:
            total, later = lax.optimization_barrier((total, later))
        return *gathered(total, spread(square)), later

    kept = {}

    square, pieces, send = finished(*reduced(halved[:CHUNKS], halved[CHUNKS:]), with_gather)
    halo = lax.ppermute(send, SEQ, onward)
    weights_one, wb_one, *halved = call(
        second_kernel,
        [SMEM_SPEC] * 2 + [VMEM_SPEC, HBM_SPEC, HBM_SPEC, VMEM_SPEC, HBM_SPEC] + [VMEM_SPEC] * 4,
        [pltpu.HBM((ROWS, HID), f32), array((ROWS, HID), bf16)] + wide,
        (core, starts, square, in_hbm(keys), in_hbm(targets), rate_one, in_hbm(weights_zero), *pieces),
        24,
        [grad] + renewal + fetched + [pltpu.VMEM((ROWS, HID), f32), pltpu.SemaphoreType.DMA((10,))],
        [HBM_SPEC] + [VMEM_SPEC] * (1 + 2 * CHUNKS),
    )
    kept["halo"], halved = lax.optimization_barrier((halo, halved))

    def attend(before, after):
        query, _ = lax.optimization_barrier((queries, before))
        attn = call(
            attend_kernel,
            [SMEM_SPEC] + [VMEM_SPEC] * 5,
            array((local, HD), f32),
            (meta, query, kept["halo"], keys, halo_v, values),
            20,
            [pltpu.VMEM((WIN, HD), bf16)],
        )
        kept["attn"], after = lax.optimization_barrier((attn, after))
        return after

    def apply(before, after):
        query, _ = lax.optimization_barrier((queries, before))
        outputs = call(
            apply_kernel,
            [SMEM_SPEC] + [VMEM_SPEC] * 4,
            array((local, HD), bf16),
            (meta, query, kept["attn"], wb_zero, wb_one),
            20,
            [pltpu.VMEM((TILE, HD), f32)],
        )
        kept["outputs"], after = lax.optimization_barrier((outputs, after))
        return after

    square, pieces, _ = finished(*reduced(halved[:CHUNKS], halved[CHUNKS:], attend, apply), None)
    weights_two = call(
        last_kernel,
        [SMEM_SPEC, VMEM_SPEC, HBM_SPEC] + [VMEM_SPEC] * 4,
        array((ROWS, HID), f32),
        (starts, square, in_hbm(weights_one), *pieces),
        20,
        renewal + [pltpu.VMEM((ROWS, HID), f32), pltpu.SemaphoreType.DMA((8,))],
        ANY_SPEC,
    )
    return (kept["outputs"], weights_two.reshape(1, 3, HD, HID))


def solution(mesh):
    finer = Mesh(mesh.devices.reshape(4, 4, 2, mesh.shape["head"]), ("z", "x", "core", "head"))
    tokens = P(SEQ, "head")
    weights = P("head", None, None, None)
    return jax.shard_map(
        per_device,
        mesh=finer,
        in_specs=(tokens,) * 5 + (P("head"), P(), weights),
        out_specs=(tokens, weights),
        check_vma=False,
    )
```

```python
import functools
import math

import jax
import jax.numpy as jnp
from jax import lax
from jax.experimental import pallas as pl
from jax.experimental.pallas import tpu as pltpu
from jax.sharding import Mesh
from jax.sharding import PartitionSpec as P

HEADS = 8
HD = 512
HID = 512
WIN = 512
ROWS = 3 * HD
SEQ = ("z", "x", "core")
TILE = 256
CHUNKS = 2
SHARES = 64
EARLY = 128

fast_rate = 0.01
epsilon = 1e-06
bf16 = jnp.bfloat16
f32 = jnp.float32
VMEM_SPEC = pl.BlockSpec(memory_space=pltpu.VMEM)
SMEM_SPEC = pl.BlockSpec(memory_space=pltpu.SMEM)
ANY_SPEC = pl.BlockSpec(memory_space=pl.ANY)
HBM_SPEC = pl.BlockSpec(memory_space=pltpu.HBM)


def dot(a, b, over_a, over_b):
    return lax.dot_general(a, b, (((over_a,), (over_b,)), ((), ())), preferred_element_type=f32)


def exchange(value, mesh_axes, partner):
    count = math.prod(lax.axis_size(a) for a in mesh_axes)
    return lax.ppermute(value, mesh_axes, [(i, partner(i)) for i in range(count)])


def ring_pair(step):
    def partner(i):
        place, core = divmod(i, 2)
        return (place ^ (1 if core == step else 3)) * 2 + core

    return partner


def swap_x(value, step):
    return exchange(value, ("x", "core"), ring_pair(step))


def swap_z(value, step):
    return exchange(value, ("z", "core"), ring_pair(step))


def swap_core(value):
    return exchange(value, ("core",), lambda i: i ^ 1)


def spread(squares):
    return lax.all_to_all(squares, ("x", "core", "head"), 0, 0, tiled=True)


def rows_of(value, start, count):
    return lax.dynamic_slice_in_dim(value, start, count, 0)


def halves():
    core = lax.axis_index("core")
    place = lax.axis_index("x")
    low, high = place & 1, place >> 1
    first = jnp.where(core == 0, low ^ high, high)
    second = jnp.where(core == 0, high, low ^ high)
    return core, first, second


def piece_starts():
    core, a, b = halves()
    here = [(a, b), (a, 1 - b), (1 - a, b), (1 - a, 1 - b)]
    there = [(b, a), (b, 1 - a), (1 - b, a), (1 - b, 1 - a)]
    places = [core * 4 + i * 2 + j for i, j in here] + [(1 - core) * 4 + i * 2 + j for i, j in there]
    return (jnp.stack(places) * (ROWS // 8)).astype(jnp.int32)


def reduced(sent, own, beside_first=None, beside_second=None):
    _, first, second = halves()
    half, rows = ROWS // 4, ROWS // 8
    chunks = range(len(sent))
    got = [swap_core(s) for s in sent]

    def two(c, start, count):
        return rows_of(own[c], start, count) + rows_of(got[c], start, count).astype(f32)

    got_x = [swap_x(two(c, (1 - first) * half, half).astype(bf16), 0) for c in chunks]
    away = (1 - second) * rows
    send = [(two(c, first * half + away, rows) + rows_of(got_x[c], away, rows).astype(f32)).astype(bf16) for c in chunks]
    got_x2 = [swap_x(s, 1) for s in send]
    near = second * rows
    mine = [two(c, first * half + near, rows) + rows_of(got_x[c], near, rows).astype(f32) + got_x2[c].astype(f32) for c in chunks]
    mine = [m.astype(bf16) for m in mine]
    other = [swap_z(m, 0) for m in mine]
    if beside_first is not None:
        other = beside_first(mine, other)
    mine = [(m.astype(f32) + o.astype(f32)).astype(bf16) for m, o in zip(mine, other)]
    other = [swap_z(m, 1) for m in mine]
    if beside_second is not None:
        other = beside_second(mine, other)
    return mine, other


def gathered(own, squares):
    near = swap_x(own, 1)
    pair = jnp.concatenate([own, near], axis=0)
    far = swap_x(pair, 0)
    far, squares = lax.optimization_barrier((far, squares))
    return squares, [pair, far, swap_core(pair), swap_core(far)]


def finish_kernel(*refs):
    total_ref, square_hbm, square_ref, sem = refs[2 * CHUNKS :]
    wide = HID // CHUNKS
    for c in range(CHUNKS):
        total = refs[c][...].astype(f32) + refs[CHUNKS + c][...].astype(f32)
        total_ref[:, c * wide : (c + 1) * wide] = total.astype(bf16)
        square = jnp.sum(total * total, axis=0, keepdims=True)
        square = square if c == 0 else before + square
        before = square
    square_ref[...] = jnp.broadcast_to(jnp.sum(square, axis=1, keepdims=True), (8, 128))[None] + jnp.zeros(square_ref.shape, f32)
    leave = pltpu.make_async_copy(square_ref, square_hbm, sem)
    leave.start()
    leave.wait()


def fetch(sources, targets, sem):
    copies = [pltpu.make_async_copy(a, b, sem.at[i]) for i, (a, b) in enumerate(zip(sources, targets))]
    for copy in copies:
        copy.start()
    return copies


def grads(place, keys_ref, targets_ref, rate_ref, wb_ref, grad_ref, outs):
    keys = keys_ref[...]
    d_out = (-rate_ref[...] * targets_ref[...].astype(f32)).astype(bf16)
    half, wide = ROWS // 2, HID // CHUNKS
    for c in range(CHUNKS):
        cols = slice(c * wide, (c + 1) * wide)
        first = dot(keys, wb_ref[0:HD, cols], 1, 0)
        third = dot(keys, wb_ref[HD : 2 * HD, cols], 1, 0)
        d_act = dot(d_out, wb_ref[2 * HD :, cols], 1, 0)
        sigma = jax.nn.sigmoid(first)
        swish = first * sigma
        act = (swish * third).astype(bf16)
        d_first = (d_act * third * sigma * (1.0 + first * (1.0 - sigma))).astype(bf16)
        d_third = (d_act * swish).astype(bf16)
        grad_ref[0:HD] = dot(keys, d_first, 0, 0)
        grad_ref[HD : 2 * HD] = dot(keys, d_third, 0, 0)
        grad_ref[2 * HD :] = dot(d_out, act, 0, 0)
        outs[c][...] = grad_ref[pl.ds(pl.multiple_of((1 - place) * half, half), half)].astype(bf16)
        outs[CHUNKS + c][...] = grad_ref[pl.ds(pl.multiple_of(place * half, half), half)]


def first_kernel(place_ref, keys_hbm, targets_hbm, values_hbm, rate_ref, w_hbm, wb_hbm, mid_hbm, late_hbm, *rest):
    outs, (grad_ref, keys_ref, targets_ref, w_ref, wb_ref, tail_ref, sem) = rest[: 2 * CHUNKS], rest[2 * CHUNKS :]
    thirds = [pl.ds(i * HD, HD) for i in range(3)]
    copies = fetch(
        [w_hbm.at[t] for t in thirds] + [keys_hbm, targets_hbm],
        [w_ref.at[t] for t in thirds] + [keys_ref, targets_ref],
        sem,
    )
    tail = keys_hbm.shape[0] - WIN
    tail_copy = pltpu.make_async_copy(values_hbm.at[pl.ds(tail, WIN)], tail_ref, sem.at[9])
    tail_copy.start()
    tails = [
        (keys_ref.at[pl.ds(tail, WIN)], mid_hbm.at[pl.ds(0, WIN)]),
        (tail_ref.at[pl.ds(0, EARLY)], mid_hbm.at[pl.ds(WIN, EARLY)]),
        (tail_ref.at[pl.ds(EARLY, WIN - EARLY)], late_hbm),
    ]
    moves = [pltpu.make_async_copy(a, b, sem.at[6 + i]) for i, (a, b) in enumerate(tails)]
    for copy, third in zip(copies, thirds):
        copy.wait()
        wb_ref[third] = w_ref[third].astype(bf16)
    leave = pltpu.make_async_copy(wb_ref, wb_hbm, sem.at[5])
    leave.start()
    copies[3].wait()
    copies[4].wait()
    tail_copy.wait()
    for move in moves:
        move.start()
    grads(place_ref[0], keys_ref, targets_ref, rate_ref, wb_ref, grad_ref, outs)
    leave.wait()
    for move in moves:
        move.wait()


def piece_rows(starts_ref):
    rows = ROWS // 8
    return [pl.ds(pl.multiple_of(starts_ref[i], rows), rows) for i in range(8)]


def renew(starts_ref, square_ref, w_ref, pieces, new_ref, out_ref, sem, wb_ref=None, arrive=None):
    mean = jnp.sum(square_ref[...], axis=0)[0:1, 0:1] / float(HEADS * ROWS * HID)
    factor = fast_rate / jnp.sqrt(mean + epsilon)
    rows = ROWS // 8
    copies = []
    for i, at in enumerate(piece_rows(starts_ref)):
        if arrive is not None:
            arrive[i].wait()
        new = w_ref[at] - factor * pieces[i // 2][i % 2 * rows : (i % 2 + 1) * rows].astype(f32)
        new_ref[at] = new
        copies.append(pltpu.make_async_copy(new_ref.at[at], out_ref.at[at], sem.at[i]))
        copies[-1].start()
        if wb_ref is not None:
            wb_ref[at] = new.astype(bf16)
    return copies


def second_kernel(place_ref, starts_ref, square_ref, keys_hbm, targets_hbm, rate_ref, w_hbm, *rest):
    pieces, (out_ref, wb_ref, *outs) = rest[:4], rest[4 : 6 + 2 * CHUNKS]
    grad_ref, new_ref, sem, keys_ref, targets_ref, w_ref, fetched = rest[6 + 2 * CHUNKS :]
    spans = piece_rows(starts_ref)
    arrive = fetch(
        [w_hbm.at[at] for at in spans] + [keys_hbm, targets_hbm],
        [w_ref.at[at] for at in spans] + [keys_ref, targets_ref],
        fetched,
    )
    copies = renew(starts_ref, square_ref, w_ref, pieces, new_ref, out_ref, sem, wb_ref, arrive)
    for copy in arrive[8:]:
        copy.wait()
    grads(place_ref[0], keys_ref, targets_ref, rate_ref, wb_ref, grad_ref, outs)
    for copy in copies:
        copy.wait()


def last_kernel(starts_ref, square_ref, w_hbm, *rest):
    pieces, (out_ref, new_ref, sem, w_ref, fetched) = rest[:4], rest[4:]
    spans = piece_rows(starts_ref)
    arrive = fetch([w_hbm.at[at] for at in spans], [w_ref.at[at] for at in spans], fetched)
    for copy in renew(starts_ref, square_ref, w_ref, pieces, new_ref, out_ref, sem, None, arrive):
        copy.wait()


def attend_kernel(meta_ref, q_ref, halo_ref, k_ref, late_v_ref, v_ref, out_ref, halo_v_ref):
    local = q_ref.shape[0]
    anchor, width = meta_ref[0], meta_ref[1]
    scale = HD ** (-0.5)
    halo_v_ref[0:EARLY] = halo_ref[WIN:]
    halo_v_ref[EARLY:] = late_v_ref[...]
    held = [(halo_ref, halo_v_ref, -WIN, WIN), (k_ref, v_ref, 0, local)]
    for start in range(0, local, TILE):
        spans = []
        for keys, values, base, count in held:
            low, high = max(base, start - WIN), min(base + count, start + TILE)
            if low < high:
                spans.append((keys, values, low - base, high - base, low))
        query = q_ref[start : start + TILE]
        scores = []
        for keys, _, low, high, position in spans:
            s = dot(query, keys[low:high], 1, 1) * scale
            row = lax.broadcasted_iota(jnp.int32, s.shape, 0) + start
            col = lax.broadcasted_iota(jnp.int32, s.shape, 1) + position
            live = (col <= row) & (col > row - width) & (col >= -anchor)
            scores.append(jnp.where(live, s, -1e30))
        peak = functools.reduce(jnp.maximum, [jnp.max(s, axis=1, keepdims=True) for s in scores])
        expo = [jnp.exp(s - peak) for s in scores]
        total = sum(jnp.sum(e, axis=1, keepdims=True) for e in expo)
        inverse = 1.0 / total
        attn = 0.0
        for e, (_, values, low, high, _) in zip(expo, spans):
            attn = attn + dot((e * inverse).astype(bf16), values[low:high], 1, 0)
        out_ref[start : start + TILE] = attn


def apply_kernel(meta_ref, q_ref, attn_ref, early_ref, late_ref, out_ref, y_ref):
    anchor, split = meta_ref[0], meta_ref[2]

    def fast(query, wb_ref):
        first = dot(query, wb_ref[0:HD], 1, 0)
        third = dot(query, wb_ref[HD : 2 * HD], 1, 0)
        act = (first * jax.nn.sigmoid(first) * third).astype(bf16)
        return dot(act, wb_ref[2 * HD :], 1, 1)

    def tile(i, carry):
        start = pl.multiple_of(i * TILE, TILE)
        rows = pl.ds(start, TILE)

        @pl.when(anchor + start < split)
        def _():
            y_ref[...] = fast(q_ref[rows], early_ref)

        @pl.when(anchor + start + TILE > split)
        def _():
            late = fast(q_ref[rows], late_ref)
            position = anchor + start + lax.broadcasted_iota(jnp.int32, late.shape, 0)
            y_ref[...] = jnp.where(position < split, y_ref[...], late)

        y = y_ref[...]
        norm = y / jnp.sqrt(jnp.mean(y * y, axis=1, keepdims=True) + epsilon)
        out_ref[rows] = (attn_ref[rows] + norm).astype(bf16)
        return carry

    lax.fori_loop(0, q_ref.shape[0] // TILE, tile, 0)


def call(kernel, specs, outs, args, megabytes, scratch=(), out_specs=None):
    return pl.pallas_call(
        kernel,
        out_shape=outs,
        in_specs=specs,
        out_specs=jax.tree.map(lambda _: VMEM_SPEC, outs) if out_specs is None else out_specs,
        scratch_shapes=list(scratch),
        compiler_params=pltpu.CompilerParams(vmem_limit_bytes=megabytes << 20),
    )(*args)


def in_hbm(value):
    return pltpu.with_memory_space_constraint(value, pltpu.HBM)


def array(shape, dtype):
    return jax.ShapeDtypeStruct(shape, dtype)


def per_device(queries, keys, values, targets, token_rate, window, split, fast_init):
    local = queries.shape[0]
    anchor = lax.axis_index(SEQ) * local
    count = lax.axis_size(SEQ)
    onward = [(i, i + 1) for i in range(count - 1)]
    positions = anchor + jnp.arange(local, dtype=jnp.int32)[:, None]
    first_block = (positions < split[0]).astype(f32)
    rate_zero = token_rate * first_block
    rate_one = token_rate * (1.0 - first_block)
    core = lax.axis_index("core").astype(jnp.int32).reshape(1)
    starts = piece_starts()
    meta = jnp.stack([anchor, window[0], split[0]]).astype(jnp.int32)
    weights_zero = fast_init.reshape(ROWS, HID)
    half = ROWS // 2
    wide = [array((half, HID // CHUNKS), kind) for kind in (bf16, f32) for _ in range(CHUNKS)]
    grad = pltpu.VMEM((ROWS, HID // CHUNKS), f32)
    renewal = [pltpu.VMEM((ROWS, HID), f32), pltpu.SemaphoreType.DMA((8,))]

    fetched = [pltpu.VMEM((local, HD), bf16)] * 2

    wb_zero, with_gather, late, *halved = call(
        first_kernel,
        [SMEM_SPEC, HBM_SPEC, HBM_SPEC, HBM_SPEC, VMEM_SPEC, HBM_SPEC],
        [pltpu.HBM((ROWS, HID), bf16), pltpu.HBM((WIN + EARLY, HD), bf16), pltpu.HBM((WIN - EARLY, HD), bf16)] + wide,
        (core, in_hbm(keys), in_hbm(targets), in_hbm(values), rate_zero, in_hbm(weights_zero)),
        24,
        [grad] + fetched + [pltpu.VMEM((ROWS, HID), f32), pltpu.VMEM((ROWS, HID), bf16), pltpu.VMEM((WIN, HD), bf16), pltpu.SemaphoreType.DMA((10,))],
        [HBM_SPEC] * 3 + [VMEM_SPEC] * (2 * CHUNKS),
    )
    halo_v = lax.ppermute(late, SEQ, onward)

    def finished(mine, other, later):
        total, square = call(
            finish_kernel,
            [VMEM_SPEC] * (2 * CHUNKS),
            [array((ROWS // 8, HID), bf16), pltpu.HBM((SHARES, 8, 128), f32)],
            (*mine, *other),
            8,
            [pltpu.VMEM((SHARES, 8, 128), f32), pltpu.SemaphoreType.DMA],
            [VMEM_SPEC, HBM_SPEC],
        )
        if later is not None:
            total, later = lax.optimization_barrier((total, later))
        return *gathered(total, spread(square)), later

    kept = {}

    square, pieces, send = finished(*reduced(halved[:CHUNKS], halved[CHUNKS:]), with_gather)
    halo = lax.ppermute(send, SEQ, onward)
    weights_one, wb_one, *halved = call(
        second_kernel,
        [SMEM_SPEC] * 2 + [VMEM_SPEC, HBM_SPEC, HBM_SPEC, VMEM_SPEC, HBM_SPEC] + [VMEM_SPEC] * 4,
        [pltpu.HBM((ROWS, HID), f32), array((ROWS, HID), bf16)] + wide,
        (core, starts, square, in_hbm(keys), in_hbm(targets), rate_one, in_hbm(weights_zero), *pieces),
        24,
        [grad] + renewal + fetched + [pltpu.VMEM((ROWS, HID), f32), pltpu.SemaphoreType.DMA((10,))],
        [HBM_SPEC] + [VMEM_SPEC] * (1 + 2 * CHUNKS),
    )
    kept["halo"], halved = lax.optimization_barrier((halo, halved))

    def attend(before, after):
        query, _ = lax.optimization_barrier((queries, before))
        attn = call(
            attend_kernel,
            [SMEM_SPEC] + [VMEM_SPEC] * 5,
            array((local, HD), f32),
            (meta, query, kept["halo"], keys, halo_v, values),
            20,
            [pltpu.VMEM((WIN, HD), bf16)],
        )
        kept["attn"], after = lax.optimization_barrier((attn, after))
        return after

    def apply(before, after):
        query, _ = lax.optimization_barrier((queries, before))
        outputs = call(
            apply_kernel,
            [SMEM_SPEC] + [VMEM_SPEC] * 4,
            array((local, HD), bf16),
            (meta, query, kept["attn"], wb_zero, wb_one),
            20,
            [pltpu.VMEM((TILE, HD), f32)],
        )
        kept["outputs"], after = lax.optimization_barrier((outputs, after))
        return after

    square, pieces, _ = finished(*reduced(halved[:CHUNKS], halved[CHUNKS:], attend, apply), None)
    weights_two = call(
        last_kernel,
        [SMEM_SPEC, VMEM_SPEC, HBM_SPEC] + [VMEM_SPEC] * 4,
        array((ROWS, HID), f32),
        (starts, square, in_hbm(weights_one), *pieces),
        20,
        renewal + [pltpu.VMEM((ROWS, HID), f32), pltpu.SemaphoreType.DMA((8,))],
        ANY_SPEC,
    )
    return (kept["outputs"], weights_two.reshape(1, 3, HD, HID))


def solution(mesh):
    finer = Mesh(mesh.devices.reshape(4, 4, 2, mesh.shape["head"]), ("z", "x", "core", "head"))
    tokens = P(SEQ, "head")
    weights = P("head", None, None, None)
    return jax.shard_map(
        per_device,
        mesh=finer,
        in_specs=(tokens,) * 5 + (P("head"), P(), weights),
        out_specs=(tokens, weights),
        check_vma=False,
    )
```

```python
import functools
import math

import jax
import jax.numpy as jnp
from jax import lax
from jax.experimental import pallas as pl
from jax.experimental.pallas import tpu as pltpu
from jax.sharding import Mesh
from jax.sharding import PartitionSpec as P

HEADS = 8
HD = 512
HID = 512
WIN = 512
ROWS = 3 * HD
SEQ = ("z", "x", "core")
TILE = 256
CHUNKS = 2
SHARES = 64
EARLY = 32

fast_rate = 0.01
epsilon = 1e-06
bf16 = jnp.bfloat16
f32 = jnp.float32
VMEM_SPEC = pl.BlockSpec(memory_space=pltpu.VMEM)
SMEM_SPEC = pl.BlockSpec(memory_space=pltpu.SMEM)
ANY_SPEC = pl.BlockSpec(memory_space=pl.ANY)
HBM_SPEC = pl.BlockSpec(memory_space=pltpu.HBM)


def dot(a, b, over_a, over_b):
    return lax.dot_general(a, b, (((over_a,), (over_b,)), ((), ())), preferred_element_type=f32)


def exchange(value, mesh_axes, partner):
    count = math.prod(lax.axis_size(a) for a in mesh_axes)
    return lax.ppermute(value, mesh_axes, [(i, partner(i)) for i in range(count)])


def ring_pair(step):
    def partner(i):
        place, core = divmod(i, 2)
        return (place ^ (1 if core == step else 3)) * 2 + core

    return partner


def swap_x(value, step):
    return exchange(value, ("x", "core"), ring_pair(step))


def swap_z(value, step):
    return exchange(value, ("z", "core"), ring_pair(step))


def swap_core(value):
    return exchange(value, ("core",), lambda i: i ^ 1)


def spread(squares):
    return lax.all_to_all(squares, ("x", "core", "head"), 0, 0, tiled=True)


def rows_of(value, start, count):
    return lax.dynamic_slice_in_dim(value, start, count, 0)


def halves():
    core = lax.axis_index("core")
    place = lax.axis_index("x")
    low, high = place & 1, place >> 1
    first = jnp.where(core == 0, low ^ high, high)
    second = jnp.where(core == 0, high, low ^ high)
    return core, first, second


def piece_starts():
    core, a, b = halves()
    here = [(a, b), (a, 1 - b), (1 - a, b), (1 - a, 1 - b)]
    there = [(b, a), (b, 1 - a), (1 - b, a), (1 - b, 1 - a)]
    places = [core * 4 + i * 2 + j for i, j in here] + [(1 - core) * 4 + i * 2 + j for i, j in there]
    return (jnp.stack(places) * (ROWS // 8)).astype(jnp.int32)


def reduced(sent, own, beside_first=None, beside_second=None):
    _, first, second = halves()
    half, rows = ROWS // 4, ROWS // 8
    chunks = range(len(sent))
    got = [swap_core(s) for s in sent]

    def two(c, start, count):
        return rows_of(own[c], start, count) + rows_of(got[c], start, count).astype(f32)

    got_x = [swap_x(two(c, (1 - first) * half, half).astype(bf16), 0) for c in chunks]
    away = (1 - second) * rows
    send = [(two(c, first * half + away, rows) + rows_of(got_x[c], away, rows).astype(f32)).astype(bf16) for c in chunks]
    got_x2 = [swap_x(s, 1) for s in send]
    near = second * rows
    mine = [two(c, first * half + near, rows) + rows_of(got_x[c], near, rows).astype(f32) + got_x2[c].astype(f32) for c in chunks]
    mine = [m.astype(bf16) for m in mine]
    other = [swap_z(m, 0) for m in mine]
    if beside_first is not None:
        other = beside_first(mine, other)
    mine = [(m.astype(f32) + o.astype(f32)).astype(bf16) for m, o in zip(mine, other)]
    other = [swap_z(m, 1) for m in mine]
    if beside_second is not None:
        other = beside_second(mine, other)
    return mine, other


def gathered(own, squares):
    near = swap_x(own, 1)
    pair = jnp.concatenate([own, near], axis=0)
    far = swap_x(pair, 0)
    far, squares = lax.optimization_barrier((far, squares))
    return squares, [pair, far, swap_core(pair), swap_core(far)]


def finish_kernel(*refs):
    total_ref, square_hbm, square_ref, sem = refs[2 * CHUNKS :]
    wide = HID // CHUNKS
    for c in range(CHUNKS):
        total = refs[c][...].astype(f32) + refs[CHUNKS + c][...].astype(f32)
        total_ref[:, c * wide : (c + 1) * wide] = total.astype(bf16)
        square = jnp.sum(total * total, axis=0, keepdims=True)
        square = square if c == 0 else before + square
        before = square
    square_ref[...] = jnp.broadcast_to(jnp.sum(square, axis=1, keepdims=True), (8, 128))[None] + jnp.zeros(square_ref.shape, f32)
    leave = pltpu.make_async_copy(square_ref, square_hbm, sem)
    leave.start()
    leave.wait()


def fetch(sources, targets, sem):
    copies = [pltpu.make_async_copy(a, b, sem.at[i]) for i, (a, b) in enumerate(zip(sources, targets))]
    for copy in copies:
        copy.start()
    return copies


def grads(place, keys_ref, targets_ref, rate_ref, wb_ref, grad_ref, outs):
    keys = keys_ref[...]
    d_out = (-rate_ref[...] * targets_ref[...].astype(f32)).astype(bf16)
    half, wide = ROWS // 2, HID // CHUNKS
    for c in range(CHUNKS):
        cols = slice(c * wide, (c + 1) * wide)
        first = dot(keys, wb_ref[0:HD, cols], 1, 0)
        third = dot(keys, wb_ref[HD : 2 * HD, cols], 1, 0)
        d_act = dot(d_out, wb_ref[2 * HD :, cols], 1, 0)
        sigma = jax.nn.sigmoid(first)
        swish = first * sigma
        act = (swish * third).astype(bf16)
        d_first = (d_act * third * sigma * (1.0 + first * (1.0 - sigma))).astype(bf16)
        d_third = (d_act * swish).astype(bf16)
        grad_ref[0:HD] = dot(keys, d_first, 0, 0)
        grad_ref[HD : 2 * HD] = dot(keys, d_third, 0, 0)
        grad_ref[2 * HD :] = dot(d_out, act, 0, 0)
        outs[c][...] = grad_ref[pl.ds(pl.multiple_of((1 - place) * half, half), half)].astype(bf16)
        outs[CHUNKS + c][...] = grad_ref[pl.ds(pl.multiple_of(place * half, half), half)]


def first_kernel(place_ref, keys_hbm, targets_hbm, values_hbm, rate_ref, w_hbm, wb_hbm, mid_hbm, late_hbm, *rest):
    outs, (grad_ref, keys_ref, targets_ref, w_ref, wb_ref, tail_ref, sem) = rest[: 2 * CHUNKS], rest[2 * CHUNKS :]
    thirds = [pl.ds(i * HD, HD) for i in range(3)]
    copies = fetch(
        [w_hbm.at[t] for t in thirds] + [keys_hbm, targets_hbm],
        [w_ref.at[t] for t in thirds] + [keys_ref, targets_ref],
        sem,
    )
    tail = keys_hbm.shape[0] - WIN
    tail_copy = pltpu.make_async_copy(values_hbm.at[pl.ds(tail, WIN)], tail_ref, sem.at[9])
    tail_copy.start()
    tails = [
        (keys_ref.at[pl.ds(tail, WIN)], mid_hbm.at[pl.ds(0, WIN)]),
        (tail_ref.at[pl.ds(0, EARLY)], mid_hbm.at[pl.ds(WIN, EARLY)]),
        (tail_ref.at[pl.ds(EARLY, WIN - EARLY)], late_hbm),
    ]
    moves = [pltpu.make_async_copy(a, b, sem.at[6 + i]) for i, (a, b) in enumerate(tails)]
    for copy, third in zip(copies, thirds):
        copy.wait()
        wb_ref[third] = w_ref[third].astype(bf16)
    leave = pltpu.make_async_copy(wb_ref, wb_hbm, sem.at[5])
    leave.start()
    copies[3].wait()
    copies[4].wait()
    tail_copy.wait()
    for move in moves:
        move.start()
    grads(place_ref[0], keys_ref, targets_ref, rate_ref, wb_ref, grad_ref, outs)
    leave.wait()
    for move in moves:
        move.wait()


def piece_rows(starts_ref):
    rows = ROWS // 8
    return [pl.ds(pl.multiple_of(starts_ref[i], rows), rows) for i in range(8)]


def renew(starts_ref, square_ref, w_ref, pieces, new_ref, out_ref, sem, wb_ref=None, arrive=None):
    mean = jnp.sum(square_ref[...], axis=0)[0:1, 0:1] / float(HEADS * ROWS * HID)
    factor = fast_rate / jnp.sqrt(mean + epsilon)
    rows = ROWS // 8
    copies = []
    for i, at in enumerate(piece_rows(starts_ref)):
        if arrive is not None:
            arrive[i].wait()
        new = w_ref[at] - factor * pieces[i // 2][i % 2 * rows : (i % 2 + 1) * rows].astype(f32)
        new_ref[at] = new
        copies.append(pltpu.make_async_copy(new_ref.at[at], out_ref.at[at], sem.at[i]))
        copies[-1].start()
        if wb_ref is not None:
            wb_ref[at] = new.astype(bf16)
    return copies


def second_kernel(place_ref, starts_ref, square_ref, keys_hbm, targets_hbm, rate_ref, w_hbm, *rest):
    pieces, (out_ref, wb_ref, *outs) = rest[:4], rest[4 : 6 + 2 * CHUNKS]
    grad_ref, new_ref, sem, keys_ref, targets_ref, w_ref, fetched = rest[6 + 2 * CHUNKS :]
    spans = piece_rows(starts_ref)
    arrive = fetch(
        [w_hbm.at[at] for at in spans] + [keys_hbm, targets_hbm],
        [w_ref.at[at] for at in spans] + [keys_ref, targets_ref],
        fetched,
    )
    copies = renew(starts_ref, square_ref, w_ref, pieces, new_ref, out_ref, sem, wb_ref, arrive)
    for copy in arrive[8:]:
        copy.wait()
    grads(place_ref[0], keys_ref, targets_ref, rate_ref, wb_ref, grad_ref, outs)
    for copy in copies:
        copy.wait()


def last_kernel(starts_ref, square_ref, w_hbm, *rest):
    pieces, (out_ref, new_ref, sem, w_ref, fetched) = rest[:4], rest[4:]
    spans = piece_rows(starts_ref)
    arrive = fetch([w_hbm.at[at] for at in spans], [w_ref.at[at] for at in spans], fetched)
    for copy in renew(starts_ref, square_ref, w_ref, pieces, new_ref, out_ref, sem, None, arrive):
        copy.wait()


def attend_kernel(meta_ref, q_ref, halo_ref, k_ref, late_v_ref, v_ref, out_ref, halo_v_ref):
    local = q_ref.shape[0]
    anchor, width = meta_ref[0], meta_ref[1]
    scale = HD ** (-0.5)
    halo_v_ref[0:EARLY] = halo_ref[WIN:]
    halo_v_ref[EARLY:] = late_v_ref[...]
    held = [(halo_ref, halo_v_ref, -WIN, WIN), (k_ref, v_ref, 0, local)]
    for start in range(0, local, TILE):
        spans = []
        for keys, values, base, count in held:
            low, high = max(base, start - WIN), min(base + count, start + TILE)
            if low < high:
                spans.append((keys, values, low - base, high - base, low))
        query = q_ref[start : start + TILE]
        scores = []
        for keys, _, low, high, position in spans:
            s = dot(query, keys[low:high], 1, 1) * scale
            row = lax.broadcasted_iota(jnp.int32, s.shape, 0) + start
            col = lax.broadcasted_iota(jnp.int32, s.shape, 1) + position
            live = (col <= row) & (col > row - width) & (col >= -anchor)
            scores.append(jnp.where(live, s, -1e30))
        peak = functools.reduce(jnp.maximum, [jnp.max(s, axis=1, keepdims=True) for s in scores])
        expo = [jnp.exp(s - peak) for s in scores]
        total = sum(jnp.sum(e, axis=1, keepdims=True) for e in expo)
        inverse = 1.0 / total
        attn = 0.0
        for e, (_, values, low, high, _) in zip(expo, spans):
            attn = attn + dot((e * inverse).astype(bf16), values[low:high], 1, 0)
        out_ref[start : start + TILE] = attn


def apply_kernel(meta_ref, q_ref, attn_ref, early_ref, late_ref, out_ref, y_ref):
    anchor, split = meta_ref[0], meta_ref[2]

    def fast(query, wb_ref):
        first = dot(query, wb_ref[0:HD], 1, 0)
        third = dot(query, wb_ref[HD : 2 * HD], 1, 0)
        act = (first * jax.nn.sigmoid(first) * third).astype(bf16)
        return dot(act, wb_ref[2 * HD :], 1, 1)

    def tile(i, carry):
        start = pl.multiple_of(i * TILE, TILE)
        rows = pl.ds(start, TILE)

        @pl.when(anchor + start < split)
        def _():
            y_ref[...] = fast(q_ref[rows], early_ref)

        @pl.when(anchor + start + TILE > split)
        def _():
            late = fast(q_ref[rows], late_ref)
            position = anchor + start + lax.broadcasted_iota(jnp.int32, late.shape, 0)
            y_ref[...] = jnp.where(position < split, y_ref[...], late)

        y = y_ref[...]
        norm = y / jnp.sqrt(jnp.mean(y * y, axis=1, keepdims=True) + epsilon)
        out_ref[rows] = (attn_ref[rows] + norm).astype(bf16)
        return carry

    lax.fori_loop(0, q_ref.shape[0] // TILE, tile, 0)


def call(kernel, specs, outs, args, megabytes, scratch=(), out_specs=None):
    return pl.pallas_call(
        kernel,
        out_shape=outs,
        in_specs=specs,
        out_specs=jax.tree.map(lambda _: VMEM_SPEC, outs) if out_specs is None else out_specs,
        scratch_shapes=list(scratch),
        compiler_params=pltpu.CompilerParams(vmem_limit_bytes=megabytes << 20),
    )(*args)


def in_hbm(value):
    return pltpu.with_memory_space_constraint(value, pltpu.HBM)


def array(shape, dtype):
    return jax.ShapeDtypeStruct(shape, dtype)


def per_device(queries, keys, values, targets, token_rate, window, split, fast_init):
    local = queries.shape[0]
    anchor = lax.axis_index(SEQ) * local
    count = lax.axis_size(SEQ)
    onward = [(i, i + 1) for i in range(count - 1)]
    positions = anchor + jnp.arange(local, dtype=jnp.int32)[:, None]
    first_block = (positions < split[0]).astype(f32)
    rate_zero = token_rate * first_block
    rate_one = token_rate * (1.0 - first_block)
    core = lax.axis_index("core").astype(jnp.int32).reshape(1)
    starts = piece_starts()
    meta = jnp.stack([anchor, window[0], split[0]]).astype(jnp.int32)
    weights_zero = fast_init.reshape(ROWS, HID)
    half = ROWS // 2
    wide = [array((half, HID // CHUNKS), kind) for kind in (bf16, f32) for _ in range(CHUNKS)]
    grad = pltpu.VMEM((ROWS, HID // CHUNKS), f32)
    renewal = [pltpu.VMEM((ROWS, HID), f32), pltpu.SemaphoreType.DMA((8,))]

    fetched = [pltpu.VMEM((local, HD), bf16)] * 2

    wb_zero, with_gather, late, *halved = call(
        first_kernel,
        [SMEM_SPEC, HBM_SPEC, HBM_SPEC, HBM_SPEC, VMEM_SPEC, HBM_SPEC],
        [pltpu.HBM((ROWS, HID), bf16), pltpu.HBM((WIN + EARLY, HD), bf16), pltpu.HBM((WIN - EARLY, HD), bf16)] + wide,
        (core, in_hbm(keys), in_hbm(targets), in_hbm(values), rate_zero, in_hbm(weights_zero)),
        24,
        [grad] + fetched + [pltpu.VMEM((ROWS, HID), f32), pltpu.VMEM((ROWS, HID), bf16), pltpu.VMEM((WIN, HD), bf16), pltpu.SemaphoreType.DMA((10,))],
        [HBM_SPEC] * 3 + [VMEM_SPEC] * (2 * CHUNKS),
    )
    halo_v = lax.ppermute(late, SEQ, onward)

    def finished(mine, other, later):
        total, square = call(
            finish_kernel,
            [VMEM_SPEC] * (2 * CHUNKS),
            [array((ROWS // 8, HID), bf16), pltpu.HBM((SHARES, 8, 128), f32)],
            (*mine, *other),
            8,
            [pltpu.VMEM((SHARES, 8, 128), f32), pltpu.SemaphoreType.DMA],
            [VMEM_SPEC, HBM_SPEC],
        )
        if later is not None:
            total, later = lax.optimization_barrier((total, later))
        return *gathered(total, spread(square)), later

    kept = {}

    square, pieces, send = finished(*reduced(halved[:CHUNKS], halved[CHUNKS:]), with_gather)
    halo = lax.ppermute(send, SEQ, onward)
    weights_one, wb_one, *halved = call(
        second_kernel,
        [SMEM_SPEC] * 2 + [VMEM_SPEC, HBM_SPEC, HBM_SPEC, VMEM_SPEC, HBM_SPEC] + [VMEM_SPEC] * 4,
        [pltpu.HBM((ROWS, HID), f32), array((ROWS, HID), bf16)] + wide,
        (core, starts, square, in_hbm(keys), in_hbm(targets), rate_one, in_hbm(weights_zero), *pieces),
        24,
        [grad] + renewal + fetched + [pltpu.VMEM((ROWS, HID), f32), pltpu.SemaphoreType.DMA((10,))],
        [HBM_SPEC] + [VMEM_SPEC] * (1 + 2 * CHUNKS),
    )
    kept["halo"], halved = lax.optimization_barrier((halo, halved))

    def attend(before, after):
        query, _ = lax.optimization_barrier((queries, before))
        attn = call(
            attend_kernel,
            [SMEM_SPEC] + [VMEM_SPEC] * 5,
            array((local, HD), f32),
            (meta, query, kept["halo"], keys, halo_v, values),
            20,
            [pltpu.VMEM((WIN, HD), bf16)],
        )
        kept["attn"], after = lax.optimization_barrier((attn, after))
        return after

    def apply(before, after):
        query, _ = lax.optimization_barrier((queries, before))
        outputs = call(
            apply_kernel,
            [SMEM_SPEC] + [VMEM_SPEC] * 4,
            array((local, HD), bf16),
            (meta, query, kept["attn"], wb_zero, wb_one),
            20,
            [pltpu.VMEM((TILE, HD), f32)],
        )
        kept["outputs"], after = lax.optimization_barrier((outputs, after))
        return after

    square, pieces, _ = finished(*reduced(halved[:CHUNKS], halved[CHUNKS:], attend, apply), None)
    weights_two = call(
        last_kernel,
        [SMEM_SPEC, VMEM_SPEC, HBM_SPEC] + [VMEM_SPEC] * 4,
        array((ROWS, HID), f32),
        (starts, square, in_hbm(weights_one), *pieces),
        20,
        renewal + [pltpu.VMEM((ROWS, HID), f32), pltpu.SemaphoreType.DMA((8,))],
        ANY_SPEC,
    )
    return (kept["outputs"], weights_two.reshape(1, 3, HD, HID))


def solution(mesh):
    finer = Mesh(mesh.devices.reshape(4, 4, 2, mesh.shape["head"]), ("z", "x", "core", "head"))
    tokens = P(SEQ, "head")
    weights = P("head", None, None, None)
    return jax.shard_map(
        per_device,
        mesh=finer,
        in_specs=(tokens,) * 5 + (P("head"), P(), weights),
        out_specs=(tokens, weights),
        check_vma=False,
    )
```
